128 devices in a mesh: dp: 4 (over y), ctx: 32 (over x, z, core).
Axes of the slice: x: 4, y: 4, z: 4, core: 2. Of those that a mesh axis runs over, the one named last changes fastest.
Arguments:
- x_in: bfloat16 [4, 4096, 4096], P('dp', 'ctx'), may hold values from -6 to 6
- b_in: bfloat16 [4, 4096, 128], P('dp', 'ctx'), may hold values from -6 to 6
- c_in: bfloat16 [4, 4096, 128], P('dp', 'ctx'), may hold values from -6 to 6
- log_decay: int32 [4, 4096, 64], P('dp', 'ctx'), may hold values from 0 to 14000, as said below
- w_out: bfloat16 [4096, 2048], P(('dp', 'ctx')), may hold values from -0.09375 to 0.09375
- cotangent: bfloat16 [4, 4096, 2048], P('dp', 'ctx'), may hold values from -6 to 6
Outputs:
- out: bfloat16 [4, 4096, 2048], P('dp', 'ctx')
- grad_x: bfloat16 [4, 4096, 4096], P('dp', 'ctx')
- grad_b: bfloat16 [4, 4096, 128], P('dp', 'ctx')
- gradient_c_input: bfloat16 [4, 4096, 128], P('dp', 'ctx')
The draws below stay inside these ranges and needn't reach their ends.
Inputs may be any that keep to these rules, and one draw needn't show every extreme that they name: log_decay holds each head's per-token log-decay as a whole number.
All inputs are finite; a program needn't handle non-finite values.
Results may differ from the reference program's by a relative error of at most 0.01.
Values may be sent and summed in bfloat16 or wider, within the bound.
A program may use at most 320 MiB of HBM per device.

```python
import jax
import jax.numpy as jnp
from jax import lax

HEADS = 64
HEAD_DIM = 64
STATE = 128
OUT_COLS = 2048
TOK_DEV = 128
SEQS = 4
SEQ = 4096
N_CTX = 32


def draw_log_decay(key, part):
    order = jax.random.permutation(jax.random.fold_in(key, 21), HEADS)
    slow = order < HEADS // 2
    slow_top = max(2, 40000 // SEQ)
    fast_level = jax.random.randint(jax.random.fold_in(key, 22), (HEADS,), 200, 1001)
    slow_level = jax.random.randint(jax.random.fold_in(key, 23), (HEADS,), 1, slow_top + 1)
    level = jnp.where(slow, slow_level, fast_level)
    factor = jax.random.randint(jax.random.fold_in(key, 24), (SEQS, SEQ // TOK_DEV, HEADS), 1, 5)
    block_level = level[None, None, :] * factor // 2
    wide_level = jnp.repeat(block_level, TOK_DEV, axis=1)
    raw = jax.random.randint(jax.random.fold_in(key, 25), (SEQS, SEQ, HEADS), 0, 1 << 20)
    value_entries = raw % (wide_level + 1)
    spots = jax.random.randint(jax.random.fold_in(key, 26), (SEQS, 2), 0, SEQ)
    decay_intensity = jax.random.randint(jax.random.fold_in(key, 27), (SEQS, 2, HEADS), 4500, 14000)
    picked = jax.random.randint(jax.random.fold_in(key, 28), (), 0, SEQS * 2 * HEADS)
    flat = jnp.arange(SEQS * 2 * HEADS).reshape(SEQS, 2, HEADS)
    decay_intensity = jnp.where(flat == picked, 14000, decay_intensity)
    match_count = (jnp.arange(SEQ)[None, :, None] == spots[:, None, :]).astype(jnp.int32)
    spike_amount = jnp.max(match_count[:, :, :, None] * decay_intensity[:, None, :, :], axis=2)
    return jnp.where(spike_amount > 0, spike_amount, value_entries).astype(jnp.int32)


def level_of(stream_key, dims, split, least, high):
    def one(dim, blocks):
        draws = jax.random.uniform(jax.random.fold_in(jax.random.fold_in(stream_key, 6), dim), (blocks,), jnp.float32, least / len(split), high / len(split))
        return jnp.repeat(jnp.exp(draws), dims[dim] // blocks).reshape((-1,) + (1,) * (len(dims) - dim - 1))

    gain = one(*split[0])
    for cut in split[1:]:
        gain = gain * one(*cut)
    return gain


def scatter_about(stream_key, extent, spread, bound, cuts=(), dtype=jnp.bfloat16):
    values = jax.random.normal(stream_key, extent, jnp.float32) * spread
    if len(cuts) > 0:
        values = level_of(stream_key, extent, cuts, -0.22, 0.18) * values
    return jnp.clip(values, min=-bound, max=bound).astype(dtype)


def setup_inputs(seed: int = 0) -> dict:
    arg_keys = jax.random.split(jax.random.key(seed), 7)
    x_in = scatter_about(arg_keys[0], (SEQS, SEQ, HEADS * HEAD_DIM), 1.0, 6.0, ((0, 4), (1, 32)))
    b_in = scatter_about(arg_keys[1], (SEQS, SEQ, STATE), 1.0, 6.0, ((0, 4), (1, 32)))
    c_in = scatter_about(arg_keys[2], (SEQS, SEQ, STATE), 1.0, 6.0, ((0, 4), (1, 32)))
    log_decay = draw_log_decay(jax.random.fold_in(arg_keys[6], 71), 0)
    w_out = scatter_about(arg_keys[4], (HEADS * HEAD_DIM, OUT_COLS), (HEADS * HEAD_DIM) ** -0.5, 0.09375, ((0, 128),))
    cotangent = scatter_about(arg_keys[5], (SEQS, SEQ, OUT_COLS), 1.0, 6.0, ((0, 4), (1, 32)))
    return dict(x_in=x_in, b_in=b_in, c_in=c_in, log_decay=log_decay, w_out=w_out, cotangent=cotangent)


decay_unit = 5e-5


def causal_decay(local_group):
    cum = local_group.T
    rows = cum.shape[1]
    diff = (cum[:, :, None] - cum[:, None, :]).astype(jnp.float32)
    lower = lax.broadcasted_iota(jnp.int32, (rows, rows), 0) >= lax.broadcasted_iota(jnp.int32, (rows, rows), 1)
    return jnp.where(lower[None], jnp.exp(-decay_unit * diff), jnp.float32(0.0))


def forward_inside_group(x_bf, local, scores, scale, group, width):
    rows, inner = x_bf.shape
    heads = local.shape[1]
    count = heads // group
    x_groups = x_bf.reshape(rows, count, group, width).transpose(1, 0, 2, 3)
    l_groups = local.reshape(rows, count, group).transpose(1, 0, 2)

    def one_group(carry, item):
        x_part, l_part = item
        mix = (scale * scores[None] * causal_decay(l_part)).astype(jnp.bfloat16)
        part = jnp.einsum("gtr,rgp->tgp", mix, x_part, preferred_element_type=jnp.float32)
        return carry, (mix, part)

    _, (mixes, parts) = lax.scan(one_group, jnp.zeros((), jnp.float32), (x_groups, l_groups))
    return mixes, parts.transpose(1, 0, 2, 3).reshape(rows, inner)


def backward_intra(mixes, x_bf, back_bf, local, scale, group, width):
    rows, inner = x_bf.shape
    heads = local.shape[1]
    count = heads // group
    x_groups = x_bf.reshape(rows, count, group, width).transpose(1, 0, 2, 3)
    d_groups = back_bf.reshape(rows, count, group, width).transpose(1, 0, 2, 3)
    l_groups = local.reshape(rows, count, group).transpose(1, 0, 2)

    def one_group(total, item):
        mix, x_part, d_part, l_part = item
        flowed = jnp.einsum("gtr,tgp->rgp", mix, d_part, preferred_element_type=jnp.float32)
        inner_prod = jnp.einsum("tgp,rgp->gtr", d_part, x_part, preferred_element_type=jnp.float32)
        total = total + jnp.sum(scale * causal_decay(l_part) * inner_prod, axis=0)
        return total, flowed

    kernel, flows = lax.scan(one_group, jnp.zeros((rows, rows), jnp.float32), (mixes, x_groups, d_groups, l_groups))
    return kernel, flows.transpose(1, 0, 2, 3).reshape(rows, inner)


def factors(local, totals, width):
    fall = jnp.exp(-decay_unit * local.astype(jnp.float32))
    tail = jnp.exp(-decay_unit * (totals[None, :] - local).astype(jnp.float32))
    return jnp.repeat(fall, width, axis=1), jnp.repeat(tail, width, axis=1)


def reference(x_in, b_in, c_in, log_decay, w_out, cotangent):
    scale = (STATE * SEQ) ** -0.5
    inner = HEADS * HEAD_DIM
    group = 8 if HEADS % 8 == 0 else HEADS
    outs, grads_x, grads_b, grads_c = [], [], [], []
    for seq in range(SEQS):
        steps = log_decay[seq].reshape(N_CTX, TOK_DEV, HEADS)
        local = jnp.cumsum(steps, axis=1).astype(jnp.int32)
        totals = local[:, -1, :]
        decays = jnp.exp(-decay_unit * totals.astype(jnp.float32))
        blocks = (x_in[seq].reshape(N_CTX, TOK_DEV, inner), b_in[seq].reshape(N_CTX, TOK_DEV, STATE), c_in[seq].reshape(N_CTX, TOK_DEV, STATE), local, totals, decays)

        def forward(before, item):
            x_bf, b_blk, c_blk, loc, tot, dec = item
            fall_wide, tail_wide = factors(loc, tot, HEAD_DIM)
            scores = jnp.dot(c_blk, b_blk.T, preferred_element_type=jnp.float32)
            mixes, y_intra = forward_inside_group(x_bf, loc, scores, scale, group, HEAD_DIM)
            before_bf = before.astype(jnp.bfloat16)
            mixed = (y_intra + scale * fall_wide * jnp.dot(c_blk, before_bf, preferred_element_type=jnp.float32)).astype(jnp.bfloat16)
            shifted = (x_bf * tail_wide).astype(jnp.bfloat16)
            term = jnp.dot(b_blk.T, shifted, preferred_element_type=jnp.float32)
            carried = jnp.repeat(dec, HEAD_DIM)[None, :] * before + term
            return carried, (mixed, shifted, before_bf)

        _, (mixed, shifted, befores) = lax.scan(forward, jnp.zeros((STATE, inner), jnp.float32), blocks)
        outs.append(jnp.dot(mixed.reshape(SEQ, inner), w_out, preferred_element_type=jnp.float32).astype(jnp.bfloat16))
        back = lax.dot_general(cotangent[seq], w_out, (((1,), (1,)), ((), ())), preferred_element_type=jnp.float32).astype(jnp.bfloat16)
        back = back.reshape(N_CTX, TOK_DEV, inner)

        def backward(after, item):
            x_bf, b_blk, c_blk, loc, tot, dec, back_bf, shifted_bfloat, before_bf = item
            fall_wide, tail_wide = factors(loc, tot, HEAD_DIM)
            scores = jnp.dot(c_blk, b_blk.T, preferred_element_type=jnp.float32)
            mixes, _ = forward_inside_group(x_bf, loc, scores, scale, group, HEAD_DIM)
            dshift = (back_bf * fall_wide).astype(jnp.bfloat16)
            after_bf = after.astype(jnp.bfloat16)
            kernel, dx_intra = backward_intra(mixes, x_bf, back_bf, loc, scale, group, HEAD_DIM)
            kernel_bf = kernel.astype(jnp.bfloat16)
            grad_x = (dx_intra + scale * tail_wide * jnp.dot(b_blk, after_bf, preferred_element_type=jnp.float32)).astype(jnp.bfloat16)
            grad_b = (jnp.dot(kernel_bf.T, c_blk, preferred_element_type=jnp.float32) + scale * jnp.dot(shifted_bfloat, after_bf.T, preferred_element_type=jnp.float32)).astype(jnp.bfloat16)
            gradient_c_input = (jnp.dot(kernel_bf, b_blk, preferred_element_type=jnp.float32) + scale * jnp.dot(dshift, before_bf.T, preferred_element_type=jnp.float32)).astype(jnp.bfloat16)
            term = jnp.dot(c_blk.T, dshift, preferred_element_type=jnp.float32)
            carried = term + jnp.repeat(dec, HEAD_DIM)[None, :] * after
            return carried, (grad_x, grad_b, gradient_c_input)

        _, (gx, gb, gc) = lax.scan(backward, jnp.zeros((STATE, inner), jnp.float32), blocks + (back, shifted, befores), reverse=True)
        grads_x.append(gx.reshape(SEQ, inner))
        grads_b.append(gb.reshape(SEQ, STATE))
        grads_c.append(gc.reshape(SEQ, STATE))
    return jnp.stack(outs), jnp.stack(grads_x), jnp.stack(grads_b), jnp.stack(grads_c)
```

```python
import functools

import jax
import jax.numpy as jnp
from jax import lax
from jax.experimental import pallas as pl
from jax.experimental.pallas import tpu as pltpu
from jax.sharding import PartitionSpec as P

decay_unit = 5e-05
MESH = pl.DeviceIdType.MESH


def causal_decay(local_group):
    cum = local_group.T
    rows = cum.shape[1]
    diff = (cum[:, :, None] - cum[:, None, :]).astype(jnp.float32)
    lower = lax.broadcasted_iota(jnp.int32, (rows, rows), 0) >= lax.broadcasted_iota(
        jnp.int32, (rows, rows), 1
    )
    return jnp.where(lower[None], jnp.exp(-decay_unit * diff), jnp.float32(0.0))


def forward_inside_group(x_bf, local, scores, scale, group, width):
    rows, inner = x_bf.shape
    heads = local.shape[1]
    count = heads // group
    x_groups = x_bf.reshape(rows, count, group, width).transpose(1, 0, 2, 3)
    l_groups = local.reshape(rows, count, group).transpose(1, 0, 2)

    def forward_one_group(carry, item):
        x_part, l_part = item
        mix = (scale * scores[None] * causal_decay(l_part)).astype(jnp.bfloat16)
        part = jnp.einsum("gtr,rgp->tgp", mix, x_part, preferred_element_type=jnp.float32)
        return (carry, (mix, part))

    _, (mixes, parts) = lax.scan(
        forward_one_group, jnp.zeros((), jnp.float32), (x_groups, l_groups)
    )
    return (mixes, parts.transpose(1, 0, 2, 3).reshape(rows, inner))


def backward_intra(mixes, x_bf, back_bf, local, scale, group, width):
    rows, inner = x_bf.shape
    heads = local.shape[1]
    count = heads // group
    x_groups = x_bf.reshape(rows, count, group, width).transpose(1, 0, 2, 3)
    d_groups = back_bf.reshape(rows, count, group, width).transpose(1, 0, 2, 3)
    l_groups = local.reshape(rows, count, group).transpose(1, 0, 2)

    def backward_one_group(total, item):
        mix, x_part, d_part, l_part = item
        flowed = jnp.einsum("gtr,tgp->rgp", mix, d_part, preferred_element_type=jnp.float32)
        inner_prod = jnp.einsum("tgp,rgp->gtr", d_part, x_part, preferred_element_type=jnp.float32)
        total = total + jnp.sum(scale * causal_decay(l_part) * inner_prod, axis=0)
        return (total, flowed)

    kernel, flows = lax.scan(
        backward_one_group,
        jnp.zeros((rows, rows), jnp.float32),
        (mixes, x_groups, d_groups, l_groups),
    )
    return (kernel, flows.transpose(1, 0, 2, 3).reshape(rows, inner))


def scan_kernel(n, reverse, send, decay, out, recv, recv_decay, stage, sems):
    me = lax.axis_index("ctx")
    state = send.shape[1]
    barrier = pltpu.get_barrier_semaphore()

    def greet(i, carry):
        pl.semaphore_signal(
            barrier, inc=1, device_id={"ctx": lax.rem(me + i, n)}, device_id_type=MESH
        )
        return carry

    lax.fori_loop(1, n, greet, 0)
    pl.semaphore_wait(barrier, n - 1)

    def exchange(source, target, first):
        def copy(source_part, target_part, peer):
            return pltpu.make_async_remote_copy(
                src_ref=source_part,
                dst_ref=target_part,
                send_sem=sems.at[first],
                recv_sem=sems.at[first + 1],
                device_id={"ctx": peer},
                device_id_type=MESH,
            )

        def post(i, carry):
            peer = lax.rem(me + i, n)
            copy(source.at[peer], target.at[me], peer).start()
            return carry

        lax.fori_loop(1, n, post, 0)
        return copy(source.at[pl.ds(0, n - 1)], target.at[pl.ds(0, n - 1)], lax.rem(me + 1, n))

    decays = exchange(decay, recv_decay, 0)
    terms = exchange(send, recv, 2)
    recv_decay[me] = decay[me]
    recv[me] = send[me]
    decays.wait()
    terms.wait()

    def step(i, carry):
        k = n - 1 - i if reverse else i
        stage[k] = carry.astype(jnp.bfloat16)
        d = recv_decay[k].astype(jnp.float32)
        d = d[0:1] + d[1:2] + d[2:3]
        return d * carry + recv[k].astype(jnp.float32)

    lax.fori_loop(0, n, step, jnp.zeros((state, 128), jnp.float32))
    result = exchange(stage, out, 4)
    out[me] = stage[me]
    result.wait()


def block_scan(term, decay_rows, reverse):
    state, inner = term.shape
    n = lax.axis_size("ctx")
    send = term.astype(jnp.bfloat16).reshape(state, n, inner // n).transpose(1, 0, 2)
    vmem = pl.BlockSpec(memory_space=pltpu.VMEM)
    out = pl.pallas_call(
        functools.partial(scan_kernel, n, reverse),
        out_shape=jax.ShapeDtypeStruct(send.shape, jnp.bfloat16),
        in_specs=[vmem, vmem],
        out_specs=vmem,
        scratch_shapes=[
            pltpu.VMEM(send.shape, jnp.bfloat16),
            pltpu.VMEM(decay_rows.shape, jnp.bfloat16),
            pltpu.VMEM(send.shape, jnp.bfloat16),
            pltpu.SemaphoreType.DMA((6,)),
        ],
        compiler_params=pltpu.CompilerParams(
            collective_id=1 if reverse else 0, has_side_effects=True
        ),
        name="scan_back" if reverse else "scan_forward",
    )(send, decay_rows)
    return out.transpose(1, 0, 2).reshape(state, inner)


def body(x_in, b_in, c_in, log_decay, w_out, cotangent):
    x_bf = x_in[0]
    b_blk = b_in[0]
    c_blk = c_in[0]
    steps = log_decay[0]
    grad_out = cotangent[0]
    rows, inner = x_bf.shape
    heads = steps.shape[1]
    width = inner // heads
    n = lax.axis_size("ctx")
    length = rows * n
    scale = (b_blk.shape[1] * length) ** (-0.5)
    group = 8
    local = jnp.cumsum(steps, axis=0)
    totals = local[-1]
    whole_proj = lax.all_gather(w_out, ("dp", "ctx"), axis=0, tiled=True)
    fall_wide = jnp.repeat(jnp.exp(-decay_unit * local.astype(jnp.float32)), width, axis=1)
    tail_wide = jnp.repeat(
        jnp.exp(-decay_unit * (totals[None, :] - local).astype(jnp.float32)), width, axis=1
    )
    decay = jnp.repeat(jnp.exp(-decay_unit * totals.astype(jnp.float32)), width)
    high = lax.reduce_precision(decay, 8, 7)
    middle = lax.reduce_precision(decay - high, 8, 7)
    low = decay - high - middle
    decay_rows = jnp.stack([high, middle, low] + [jnp.zeros_like(high)] * 13)
    decay_rows = decay_rows.astype(jnp.bfloat16).reshape(16, n, inner // n).transpose(1, 0, 2)
    scores = jnp.dot(c_blk, b_blk.T, preferred_element_type=jnp.float32)
    shifted = (x_bf * tail_wide).astype(jnp.bfloat16)
    term = jnp.dot(b_blk.T, shifted, preferred_element_type=jnp.float32)
    before_bf = block_scan(term, decay_rows, False)
    mixes, y_intra = forward_inside_group(x_bf, local, scores, scale, group, width)
    mixed = (
        y_intra + scale * fall_wide * jnp.dot(c_blk, before_bf, preferred_element_type=jnp.float32)
    ).astype(jnp.bfloat16)
    out = jnp.dot(mixed, whole_proj, preferred_element_type=jnp.float32).astype(jnp.bfloat16)
    back_bf = lax.dot_general(
        grad_out, whole_proj, (((1,), (1,)), ((), ())), preferred_element_type=jnp.float32
    ).astype(jnp.bfloat16)
    dshift = (back_bf * fall_wide).astype(jnp.bfloat16)
    adjoint_term = jnp.dot(c_blk.T, dshift, preferred_element_type=jnp.float32)
    after_bf = block_scan(adjoint_term, decay_rows, True)
    kernel, dx_intra = backward_intra(mixes, x_bf, back_bf, local, scale, group, width)
    kernel_bf = kernel.astype(jnp.bfloat16)
    grad_x = (
        dx_intra + scale * tail_wide * jnp.dot(b_blk, after_bf, preferred_element_type=jnp.float32)
    ).astype(jnp.bfloat16)
    grad_b = (
        jnp.dot(kernel_bf.T, c_blk, preferred_element_type=jnp.float32)
        + scale * jnp.dot(shifted, after_bf.T, preferred_element_type=jnp.float32)
    ).astype(jnp.bfloat16)
    gradient_c_input = (
        jnp.dot(kernel_bf, b_blk, preferred_element_type=jnp.float32)
        + scale * jnp.dot(dshift, before_bf.T, preferred_element_type=jnp.float32)
    ).astype(jnp.bfloat16)
    return (out[None], grad_x[None], grad_b[None], gradient_c_input[None])


def solution(mesh):
    in_specs = (
        P("dp", "ctx", None),
        P("dp", "ctx", None),
        P("dp", "ctx", None),
        P("dp", "ctx", None),
        P(("dp", "ctx"), None),
        P("dp", "ctx", None),
    )
    out_specs = (
        P("dp", "ctx", None),
        P("dp", "ctx", None),
        P("dp", "ctx", None),
        P("dp", "ctx", None),
    )
    return jax.shard_map(body, mesh=mesh, in_specs=in_specs, out_specs=out_specs, check_vma=False)
```

```python
import functools

import jax
import jax.numpy as jnp
from jax import lax
from jax.experimental import pallas as pl
from jax.experimental.pallas import tpu as pltpu
from jax.sharding import PartitionSpec as P

decay_unit = 5e-05
rate = decay_unit * 1.4426950408889634
MESH = pl.DeviceIdType.MESH
F32 = jnp.float32
BF = jnp.bfloat16
LANES = 128


def dot(a, b):
    return lax.dot_general(a, b, (((1,), (0,)), ((), ())), preferred_element_type=F32)


def dot_nt(a, b):
    return lax.dot_general(a, b, (((1,), (1,)), ((), ())), preferred_element_type=F32)


def flip(a):
    return a.astype(F32).T


def span(j, size=LANES):
    return pl.ds(pl.multiple_of(j * size, size), size)


def grid_of(rows, columns):
    return (
        lax.broadcasted_iota(jnp.int32, (rows, columns), 0),
        lax.broadcasted_iota(jnp.int32, (rows, columns), 1),
    )


def greet_all(n):
    me = lax.axis_index("ctx")
    barrier = pltpu.get_barrier_semaphore()

    def greet(i, carry):
        pl.semaphore_signal(
            barrier, inc=1, device_id={"ctx": lax.rem(me + i, n)}, device_id_type=MESH
        )
        return carry

    lax.fori_loop(1, n, greet, 0)
    return barrier


def copy_to(peer, source, target, sems, first):
    return pltpu.make_async_remote_copy(
        src_ref=source,
        dst_ref=target,
        send_sem=sems.at[first],
        recv_sem=sems.at[first + 1],
        device_id={"ctx": peer},
        device_id_type=MESH,
    )


def finish(n, source, target, sems, first):
    peer = lax.rem(lax.axis_index("ctx") + 1, n)
    some = pl.ds(0, n - 1)
    copy_to(peer, source.at[some], target.at[some], sems, first).wait()


def accumulate_decay(steps, level):
    rows, heads = steps.shape
    row, column = grid_of(rows, rows)
    ones = jnp.where(row >= column, 1.0, 0.0).astype(BF)
    value = steps[...]
    high = (value >> 7).astype(F32).astype(BF)
    low = (value & 127).astype(F32).astype(BF)
    level[...] = jnp.zeros_like(level)
    level[:, :heads] = (dot(ones, high) * 128.0 + dot(ones, low)) * rate


def columns_of(level, j):
    rolled = pltpu.roll(level[...], lax.rem(LANES - 2 * j, LANES), 1)
    shape = rolled.shape
    return jnp.broadcast_to(rolled[:, 0:1], shape), jnp.broadcast_to(rolled[:, 1:2], shape)


def paired(level, j):
    one, two = columns_of(level, j)
    _, column = grid_of(*one.shape)
    both = jnp.where(column < LANES // 2, one, two)
    return both, both[both.shape[0] - 1 :]


def split_heads(value):
    _, column = grid_of(*value.shape)
    wide = value.astype(F32)
    left = jnp.where(column < LANES // 2, wide, 0.0).astype(BF)
    right = jnp.where(column < LANES // 2, 0.0, wide).astype(BF)
    return jnp.concatenate([left, right], axis=0)


def forward_kernel(
    n, scale, x, b, c, steps, mixed, before, level, decays, level_t, masked, b_t, y, send, recv,
    stage, sems,
):
    me = lax.axis_index("ctx")
    rows = x.shape[0]
    state = b.shape[1]
    barrier = greet_all(n)
    accumulate_decay(steps, level)
    level_t[...] = flip(level[...])
    row, column = grid_of(rows, rows)
    masked[...] = jnp.where(row >= column, scale * dot_nt(c[...], b[...]), 0.0)
    b_t[...] = flip(b[...]).astype(BF)
    pl.semaphore_wait(barrier, n - 1)

    def send_term(i, carry):
        j = lax.rem(me + i, n)
        both, last = paired(level, j)
        shifted = (x[:, span(j)].astype(F32) * jnp.exp2(both - last)).astype(BF)
        send[j, :state] = dot(b_t[...], shifted).astype(BF)
        d = jnp.exp2(-last)
        high = d.astype(BF).astype(F32)
        middle = (d - high).astype(BF).astype(F32)
        low = d - high - middle
        which, _ = grid_of(16, LANES)
        parts = jnp.where(which == 0, high, jnp.where(which == 1, middle, low))
        send[j, state:] = jnp.where(which < 3, parts, 0.0).astype(BF)

        @pl.when(i < n)
        def _():
            copy_to(j, send.at[j], recv.at[me], sems, 0).start()

        return carry

    lax.fori_loop(1, n + 1, send_term, 0)

    def inside(j, carry):
        one, two = columns_of(level, j)
        first = jnp.exp2(jnp.minimum(level_t[pl.ds(2 * j, 1), :] - one, 0.0))
        second = jnp.exp2(jnp.minimum(level_t[pl.ds(2 * j + 1, 1), :] - two, 0.0))
        mix = jnp.concatenate(
            [(masked[...] * first).astype(BF), (masked[...] * second).astype(BF)], axis=1
        )
        y[j] = dot(mix, split_heads(x[:, span(j)]))
        return carry

    lax.fori_loop(0, n // 2, inside, 0)
    recv[me] = send[me]
    finish(n, send, recv, sems, 0)

    def step(k, carry):
        stage[k] = carry.astype(BF)
        parts = recv[k, state:].astype(F32)
        d = parts[0:1] + parts[1:2] + parts[2:3]
        decays[k] = jnp.broadcast_to(d, (8, LANES))

        @pl.when(k != me)
        def _():
            copy_to(k, stage.at[k], before.at[me], sems, 2).start()

        return d * carry + recv[k, :state].astype(F32)

    lax.fori_loop(0, n, step, jnp.zeros((state, LANES), F32))
    before[me] = stage[me]
    lax.fori_loop(n // 2, n, inside, 0)
    finish(n, stage, before, sems, 2)

    def join(j, carry):
        both, _ = paired(level, j)
        carried = scale * jnp.exp2(-both) * dot(c[...], before[j])
        mixed[:, span(j)] = (y[j] + carried).astype(BF)
        return carry

    lax.fori_loop(0, n, join, 0)


def backward_kernel(
    n, scale, x, b, c, cot, mixed, before, level, decays, w, out, grad_x, grad_b, grad_c,
    level_t, masked_t, c_t, whole, back, dshift, flow, inner_sum, b_sum, c_sum, send, recv, stage,
    after, sems, w_sems,
):
    me = lax.axis_index("ctx")
    rows = x.shape[0]
    state = b.shape[1]
    chunks = w_sems.shape[0]
    depth = w.shape[0] // chunks
    each = n // chunks

    def place(i):
        return lax.rem(me // each + 1 + i, chunks)

    def fetch(i):
        part = span(place(i), depth)
        return pltpu.make_async_copy(w.at[part], whole.at[part], w_sems.at[i])

    def fetch_one(i, carry):
        fetch(i).start()
        return carry

    lax.fori_loop(0, chunks, fetch_one, 0)
    barrier = greet_all(n)
    level_t[...] = flip(level[...])
    row, column = grid_of(rows, rows)
    masked_t[...] = jnp.where(row <= column, scale * dot_nt(b[...], c[...]), 0.0)
    c_t[...] = flip(c[...]).astype(BF)
    inner_sum[...] = jnp.zeros_like(inner_sum)
    b_sum[...] = jnp.zeros_like(b_sum)
    c_sum[...] = jnp.zeros_like(c_sum)
    pl.semaphore_wait(barrier, n - 1)

    def send_term(i, carry):
        fetch(i).wait()
        q = place(i)
        part = dot_nt(cot[...], whole[span(q, depth), :]).astype(BF)
        back[:, span(q, depth)] = part
        for u in range(each):
            j = q * each + u
            both, _ = paired(level, j)
            piece = part[:, u * LANES : (u + 1) * LANES].astype(F32)
            shift = (piece * jnp.exp2(-both)).astype(BF)
            dshift[:, span(j)] = shift
            send[j] = dot(c_t[...], shift).astype(BF)

            @pl.when(j != me)
            def _():
                copy_to(j, send.at[j], recv.at[me], sems, 0).start()

        return carry

    lax.fori_loop(0, chunks, send_term, 0)

    def inside(j, carry):
        one, two = columns_of(level, j)
        first = jnp.exp2(jnp.minimum(one - level_t[pl.ds(2 * j, 1), :], 0.0))
        second = jnp.exp2(jnp.minimum(two - level_t[pl.ds(2 * j + 1, 1), :], 0.0))
        mix = jnp.concatenate(
            [(masked_t[...] * first).astype(BF), (masked_t[...] * second).astype(BF)], axis=1
        )
        part = back[:, span(j)]
        flow[j] = dot(mix, split_heads(part))
        pair = dot_nt(split_heads(x[:, span(j)]), part)
        inner_sum[...] += first * pair[:rows] + second * pair[rows:]
        c_sum[...] += dot_nt(dshift[:, span(j)], before[j])
        return carry

    lax.fori_loop(0, n, inside, 0)
    recv[me] = send[me]
    finish(n, send, recv, sems, 0)

    def step(i, carry):
        k = n - 1 - i
        stage[k] = carry.astype(BF)

        @pl.when(k != me)
        def _():
            copy_to(k, stage.at[k], after.at[me], sems, 2).start()

        return decays[k, 0:1] * carry + recv[k].astype(F32)

    lax.fori_loop(0, n, step, jnp.zeros((state, LANES), F32))
    after[me] = stage[me]

    def project(i, carry):
        out[:, span(i, 256)] = dot(mixed[...], whole[:, span(i, 256)]).astype(BF)
        return carry

    lax.fori_loop(0, out.shape[1] // 256, project, 0)
    kernel_t = jnp.where(row <= column, scale * inner_sum[...], 0.0)
    kernel = kernel_t.T.astype(BF)
    grad_c[...] = (dot(kernel, b[...]) + scale * c_sum[...]).astype(BF)
    finish(n, stage, after, sems, 2)

    def join(j, carry):
        both, last = paired(level, j)
        tail = jnp.exp2(both - last)
        grad_x[:, span(j)] = (flow[j] + scale * tail * dot(b[...], after[j])).astype(BF)
        shifted = (x[:, span(j)].astype(F32) * tail).astype(BF)
        b_sum[...] += dot_nt(shifted, after[j])
        return carry

    lax.fori_loop(0, n, join, 0)
    grad_b[...] = (dot(kernel_t.astype(BF), c[...]) + scale * b_sum[...]).astype(BF)


def body(x_in, b_in, c_in, log_decay, w_out, cotangent):
    x, b, c, steps, cot = x_in[0], b_in[0], c_in[0], log_decay[0], cotangent[0]
    rows, inner = x.shape
    state = b.shape[1]
    n = lax.axis_size("ctx")
    scale = (state * rows * n) ** (-0.5)
    vmem = pl.BlockSpec(memory_space=pltpu.VMEM)
    hbm = pl.BlockSpec(memory_space=pl.ANY)
    shape = jax.ShapeDtypeStruct
    square = pltpu.VMEM((rows, rows), F32)
    blocks = (n, state, LANES)
    whole = lax.all_gather(w_out, ("dp", "ctx"), axis=0, tiled=True)
    mixed, before, level, decays = pl.pallas_call(
        functools.partial(forward_kernel, n, scale),
        out_shape=(
            shape(x.shape, BF), shape(blocks, BF), shape((rows, LANES), F32),
            shape((n, 8, LANES), F32),
        ),
        in_specs=[vmem] * 4,
        out_specs=(vmem,) * 4,
        scratch_shapes=[
            square,
            square,
            pltpu.VMEM((state, rows), BF),
            pltpu.VMEM((n, rows, LANES), F32),
            pltpu.VMEM((n, state + 16, LANES), BF),
            pltpu.VMEM((n, state + 16, LANES), BF),
            pltpu.VMEM(blocks, BF),
            pltpu.SemaphoreType.DMA((4,)),
        ],
        compiler_params=pltpu.CompilerParams(collective_id=0, has_side_effects=True),
        cost_estimate=pl.CostEstimate(
            flops=2000000000, bytes_accessed=8000000, transcendentals=2000000
        ),
        name="forward",
    )(x, b, c, steps)
    chunks = n // 2
    results = pl.pallas_call(
        functools.partial(backward_kernel, n, scale),
        out_shape=(
            shape(cot.shape, BF), shape(x.shape, BF), shape(b.shape, BF), shape(c.shape, BF),
        ),
        in_specs=[vmem] * 8 + [hbm],
        out_specs=(vmem,) * 4,
        scratch_shapes=[
            square,
            square,
            pltpu.VMEM((state, rows), BF),
            pltpu.VMEM(whole.shape, BF),
            pltpu.VMEM(x.shape, BF),
            pltpu.VMEM(x.shape, BF),
            pltpu.VMEM((n, rows, LANES), F32),
            square,
            pltpu.VMEM((rows, state), F32),
            pltpu.VMEM((rows, state), F32),
            pltpu.VMEM(blocks, BF),
            pltpu.VMEM(blocks, BF),
            pltpu.VMEM(blocks, BF),
            pltpu.VMEM(blocks, BF),
            pltpu.SemaphoreType.DMA((4,)),
            pltpu.SemaphoreType.DMA((chunks,)),
        ],
        compiler_params=pltpu.CompilerParams(
            collective_id=1, has_side_effects=True, vmem_limit_bytes=56 * 1024 * 1024
        ),
        name="backward",
    )(x, b, c, cot, mixed, before, level, decays, whole)
    return tuple(r[None] for r in results)


def solution(mesh):
    tokens = P("dp", "ctx", None)
    return jax.shard_map(
        body,
        mesh=mesh,
        in_specs=(tokens, tokens, tokens, tokens, P(("dp", "ctx"), None), tokens),
        out_specs=(tokens, tokens, tokens, tokens),
        check_vma=False,
    )
```

```python
import functools

import jax
import jax.numpy as jnp
from jax import lax
from jax.experimental import pallas as pl
from jax.experimental.pallas import tpu as pltpu
from jax.sharding import PartitionSpec as P

decay_unit = 5e-05
rate = decay_unit * 1.4426950408889634
MESH = pl.DeviceIdType.MESH
F32 = jnp.float32
BF = jnp.bfloat16
LANES = 128
SIDE = 4
ORDERS = ((1, 0, 2), (0, 2, 1), (2, 1, 0))
CUTS = (0, 640, 1280, 2048)


def dot(a, b):
    return lax.dot_general(a, b, (((1,), (0,)), ((), ())), preferred_element_type=F32)


def dot_nt(a, b):
    return lax.dot_general(a, b, (((1,), (1,)), ((), ())), preferred_element_type=F32)


def flip(a):
    return a.astype(F32).T


def span(j, size=LANES):
    return pl.ds(pl.multiple_of(j * size, size), size)


def grid_of(rows, columns):
    return (
        lax.broadcasted_iota(jnp.int32, (rows, columns), 0),
        lax.broadcasted_iota(jnp.int32, (rows, columns), 1),
    )


def greet_all(n):
    me, seq = lax.axis_index("ctx"), lax.axis_index("dp")
    barrier = pltpu.get_barrier_semaphore()

    def greet(i, carry):
        pl.semaphore_signal(
            barrier, inc=1, device_id={"ctx": lax.rem(me + i, n)}, device_id_type=MESH
        )
        return carry

    lax.fori_loop(1, n, greet, 0)
    for turn in (1, SIDE - 1):
        pl.semaphore_signal(
            barrier, inc=1, device_id={"dp": lax.rem(seq + turn, SIDE)}, device_id_type=MESH
        )
    return barrier


def copy_to(peer, source, target, sems, first):
    return pltpu.make_async_remote_copy(
        src_ref=source,
        dst_ref=target,
        send_sem=sems.at[first],
        recv_sem=sems.at[first + 1],
        device_id={"ctx": peer},
        device_id_type=MESH,
    )


def finish(n, source, target, sems, first):
    peer = lax.rem(lax.axis_index("ctx") + 1, n)
    some = pl.ds(0, n - 1)
    copy_to(peer, source.at[some], target.at[some], sems, first).wait()


def accumulate_decay(steps, level):
    rows, heads = steps.shape
    row, column = grid_of(rows, rows)
    ones = jnp.where(row >= column, 1.0, 0.0).astype(BF)
    value = steps[...]
    high = (value >> 7).astype(F32).astype(BF)
    low = (value & 127).astype(F32).astype(BF)
    level[...] = jnp.zeros_like(level)
    level[:, :heads] = (dot(ones, high) * 128.0 + dot(ones, low)) * rate


def columns_of(level, j):
    rolled = pltpu.roll(level[...], lax.rem(LANES - 2 * j, LANES), 1)
    shape = rolled.shape
    return jnp.broadcast_to(rolled[:, 0:1], shape), jnp.broadcast_to(rolled[:, 1:2], shape)


def paired(level, j):
    one, two = columns_of(level, j)
    _, column = grid_of(*one.shape)
    both = jnp.where(column < LANES // 2, one, two)
    return both, both[both.shape[0] - 1 :]


def split_heads(value):
    _, column = grid_of(*value.shape)
    wide = value.astype(F32)
    left = jnp.where(column < LANES // 2, wide, 0.0).astype(BF)
    right = jnp.where(column < LANES // 2, 0.0, wide).astype(BF)
    return jnp.concatenate([left, right], axis=0)


class Gather:
    def __init__(self, shard, whole, own_sem, ring_send, ring_recv, pair_send, pair_recv):
        ctx = lax.axis_index("ctx")
        self.at = (lax.axis_index("dp"), ctx // (2 * SIDE), lax.rem(ctx // 2, SIDE))
        self.core = lax.rem(ctx, 2)
        self.shard, self.whole = shard, whole
        self.own_sem = own_sem
        self.ring_send, self.ring_recv = ring_send, ring_recv
        self.pair_send, self.pair_recv = pair_send, pair_recv

    def device(self, dim, place, core):
        y, x, z = [place if d == dim else v for d, v in enumerate(self.at)]
        return {"dp": y, "ctx": (x * SIDE + z) * 2 + core}

    def region(self, part, phase, place, rows):
        order = ORDERS[part]
        index = list(self.at)
        for dim in order[:phase]:
            index[dim] = slice(None)
        index[order[phase]] = place
        columns = pl.ds(CUTS[part], CUTS[part + 1] - CUTS[part])
        return self.whole.at[(*index, self.core, rows, columns)]

    def ring(self, part, phase, step):
        dim = ORDERS[part][phase]
        here = self.at[dim]
        right, left = lax.rem(here + 1, SIDE), lax.rem(here + SIDE - 1, SIDE)
        rows = self.shard.shape[0]
        for side, (peer, other) in enumerate(((right, left), (left, right))):
            if step == 0:
                piece = self.region(part, phase, here, pl.ds(0, rows))
            else:
                piece = self.region(part, phase, other, pl.ds(side * (rows // 2), rows // 2))
            yield pltpu.make_async_remote_copy(
                src_ref=piece,
                dst_ref=piece,
                send_sem=self.ring_send.at[part, phase, step, side],
                recv_sem=self.ring_recv.at[part, phase, step, side],
                device_id=self.device(dim, peer, self.core),
                device_id_type=MESH,
            )

    def pair(self, part, turn):
        dim = ORDERS[part][2]
        place = lax.rem(self.at[dim] + turn, SIDE)
        piece = self.region(part, 2, place, pl.ds(0, self.shard.shape[0]))
        return pltpu.make_async_remote_copy(
            src_ref=piece,
            dst_ref=piece,
            send_sem=self.pair_send.at[part, turn],
            recv_sem=self.pair_recv.at[part, turn],
            device_id=self.device(None, None, 1 - self.core),
            device_id_type=MESH,
        )

    def post(self, part, number):
        for copy in self.ring(part, number // 2, number % 2):
            copy.start()

    def begin(self):
        own = pltpu.make_async_copy(
            self.shard, self.whole.at[(*self.at, self.core)], self.own_sem.at[0]
        )
        own.start()
        own.wait()
        for part in range(3):
            self.post(part, 0)

    def advance(self, number):
        turns = {3: (0,), 4: (1, 3), 5: (2,)}.get(number, ())
        for part in range(3):
            for copy in self.ring(part, number // 2, number % 2):
                copy.wait()
            if number < 5:
                self.post(part, number + 1)
            for turn in turns:
                self.pair(part, turn).start()

    def end(self):
        for part in range(3):
            for turn in range(SIDE):
                self.pair(part, turn).wait()


def layer_kernel(
    n, scale, x, b, c, steps, cot, shard, out, grad_x, grad_b, grad_c,
    level, level_t, masked, masked_t, b_t, c_t, decays, y, send, recv, stage, before, mixed,
    whole, back, dshift, flow, inner_sum, b_sum, c_sum, send2, recv2, stage2, after,
    sems, own_sem, ring_send, ring_recv, pair_send, pair_recv,
):
    me = lax.axis_index("ctx")
    rows = x.shape[0]
    state = b.shape[1]
    barrier = greet_all(n)
    gather = Gather(shard, whole, own_sem, ring_send, ring_recv, pair_send, pair_recv)
    pl.semaphore_wait(barrier, n + 1)
    gather.begin()

    accumulate_decay(steps, level)
    level_t[...] = flip(level[...])
    row, column = grid_of(rows, rows)
    masked[...] = jnp.where(row >= column, scale * dot_nt(c[...], b[...]), 0.0)
    masked_t[...] = jnp.where(row <= column, scale * dot_nt(b[...], c[...]), 0.0)
    b_t[...] = flip(b[...]).astype(BF)
    c_t[...] = flip(c[...]).astype(BF)
    inner_sum[...] = jnp.zeros_like(inner_sum)
    b_sum[...] = jnp.zeros_like(b_sum)
    c_sum[...] = jnp.zeros_like(c_sum)

    def make_term(j, carry):
        both, last = paired(level, j)
        shifted = (x[:, span(j)].astype(F32) * jnp.exp2(both - last)).astype(BF)
        send[j, :state] = dot(b_t[...], shifted).astype(BF)
        d = jnp.exp2(-last)
        high = d.astype(BF).astype(F32)
        middle = (d - high).astype(BF).astype(F32)
        low = d - high - middle
        which, _ = grid_of(16, LANES)
        parts = jnp.where(which == 0, high, jnp.where(which == 1, middle, low))
        send[j, state:] = jnp.where(which < 3, parts, 0.0).astype(BF)
        return carry

    def inside(j, carry):
        one, two = columns_of(level, j)
        first = jnp.exp2(jnp.minimum(level_t[pl.ds(2 * j, 1), :] - one, 0.0))
        second = jnp.exp2(jnp.minimum(level_t[pl.ds(2 * j + 1, 1), :] - two, 0.0))
        mix = jnp.concatenate(
            [(masked[...] * first).astype(BF), (masked[...] * second).astype(BF)], axis=1
        )
        y[j] = dot(mix, split_heads(x[:, span(j)]))
        return carry

    gather.advance(0)
    lax.fori_loop(0, n // 4, make_term, 0)
    gather.advance(1)
    lax.fori_loop(n // 4, n, make_term, 0)
    gather.advance(2)
    lax.fori_loop(0, n // 4, inside, 0)
    gather.advance(3)

    def post_term(i, carry):
        j = lax.rem(me + i, n)
        copy_to(j, send.at[j], recv.at[me], sems, 0).start()
        return carry

    lax.fori_loop(1, n, post_term, 0)
    recv[me] = send[me]
    lax.fori_loop(n // 4, n, inside, 0)
    gather.advance(4)
    finish(n, send, recv, sems, 0)

    def step(k, carry):
        stage[k] = carry.astype(BF)
        parts = recv[k, state:].astype(F32)
        d = parts[0:1] + parts[1:2] + parts[2:3]
        decays[k] = jnp.broadcast_to(d, (8, LANES))

        @pl.when(k != me)
        def _():
            copy_to(k, stage.at[k], before.at[me], sems, 2).start()

        return d * carry + recv[k, :state].astype(F32)

    lax.fori_loop(0, n, step, jnp.zeros((state, LANES), F32))
    before[me] = stage[me]
    gather.advance(5)
    gather.end()

    depth = 2 * LANES

    def send_term(i, carry):
        q = lax.rem(me // 2 + 1 + i, n // 2)
        chunk = whole[q // SIDE, lax.rem(q, SIDE)].reshape(depth, cot.shape[1])
        part = dot_nt(cot[...], chunk).astype(BF)
        back[:, span(q, depth)] = part
        for u in range(2):
            j = q * 2 + u
            both, _ = paired(level, j)
            piece = part[:, u * LANES : (u + 1) * LANES].astype(F32)
            shift = (piece * jnp.exp2(-both)).astype(BF)
            dshift[:, span(j)] = shift
            send2[j] = dot(c_t[...], shift).astype(BF)

            @pl.when(j != me)
            def _():
                copy_to(j, send2.at[j], recv2.at[me], sems, 4).start()

        return carry

    lax.fori_loop(0, n // 2, send_term, 0)
    recv2[me] = send2[me]
    finish(n, stage, before, sems, 2)

    def inside_back(j, carry):
        one, two = columns_of(level, j)
        first = jnp.exp2(jnp.minimum(one - level_t[pl.ds(2 * j, 1), :], 0.0))
        second = jnp.exp2(jnp.minimum(two - level_t[pl.ds(2 * j + 1, 1), :], 0.0))
        mix = jnp.concatenate(
            [(masked_t[...] * first).astype(BF), (masked_t[...] * second).astype(BF)], axis=1
        )
        part = back[:, span(j)]
        flow[j] = dot(mix, split_heads(part))
        pair = dot_nt(split_heads(x[:, span(j)]), part)
        inner_sum[...] += first * pair[:rows] + second * pair[rows:]
        c_sum[...] += dot_nt(dshift[:, span(j)], before[j])
        return carry

    lax.fori_loop(0, n // 2, inside_back, 0)
    finish(n, send2, recv2, sems, 4)

    def step_back(i, carry):
        k = n - 1 - i
        stage2[k] = carry.astype(BF)

        @pl.when(k != me)
        def _():
            copy_to(k, stage2.at[k], after.at[me], sems, 6).start()

        return decays[k, 0:1] * carry + recv2[k].astype(F32)

    lax.fori_loop(0, n, step_back, jnp.zeros((state, LANES), F32))
    after[me] = stage2[me]
    lax.fori_loop(n // 2, n, inside_back, 0)

    def join(j, carry):
        both, _ = paired(level, j)
        carried = scale * jnp.exp2(-both) * dot(c[...], before[j])
        mixed[:, span(j)] = (y[j] + carried).astype(BF)
        return carry

    lax.fori_loop(0, n, join, 0)

    def project(i, carry):
        chunk = whole[:, :, :, :, :, span(i, 256)].reshape(x.shape[1], 256)
        out[:, span(i, 256)] = dot(mixed[...], chunk).astype(BF)
        return carry

    lax.fori_loop(0, out.shape[1] // 256, project, 0)
    kernel_t = jnp.where(row <= column, scale * inner_sum[...], 0.0)
    kernel = kernel_t.T.astype(BF)
    grad_c[...] = (dot(kernel, b[...]) + scale * c_sum[...]).astype(BF)
    finish(n, stage2, after, sems, 6)

    def join_back(j, carry):
        both, last = paired(level, j)
        tail = jnp.exp2(both - last)
        grad_x[:, span(j)] = (flow[j] + scale * tail * dot(b[...], after[j])).astype(BF)
        shifted = (x[:, span(j)].astype(F32) * tail).astype(BF)
        b_sum[...] += dot_nt(shifted, after[j])
        return carry

    lax.fori_loop(0, n, join_back, 0)
    grad_b[...] = (dot(kernel_t.astype(BF), c[...]) + scale * b_sum[...]).astype(BF)


def body(x_in, b_in, c_in, log_decay, w_out, cotangent):
    x, b, c, steps, cot = x_in[0], b_in[0], c_in[0], log_decay[0], cotangent[0]
    rows = x.shape[0]
    state = b.shape[1]
    n = lax.axis_size("ctx")
    scale = (state * rows * n) ** (-0.5)
    vmem = pl.BlockSpec(memory_space=pltpu.VMEM)
    shape = jax.ShapeDtypeStruct
    square = pltpu.VMEM((rows, rows), F32)
    turned = pltpu.VMEM((state, rows), BF)
    blocks = pltpu.VMEM((n, state, LANES), BF)
    marked = pltpu.VMEM((n, state + 16, LANES), BF)
    parts = pltpu.VMEM((n, rows, LANES), F32)
    wide = pltpu.VMEM(x.shape, BF)
    sums = pltpu.VMEM((rows, state), F32)
    ring = pltpu.SemaphoreType.DMA((3, 3, 2, 2))
    pair = pltpu.SemaphoreType.DMA((3, SIDE))
    results = pl.pallas_call(
        functools.partial(layer_kernel, n, scale),
        out_shape=(
            shape(cot.shape, BF), shape(x.shape, BF), shape(b.shape, BF), shape(c.shape, BF),
        ),
        in_specs=[vmem] * 6,
        out_specs=(vmem,) * 4,
        scratch_shapes=[
            square, square, square, square, turned, turned,
            pltpu.VMEM((n, 8, LANES), F32),
            parts, marked, marked, blocks, blocks, wide,
            pltpu.VMEM((SIDE, SIDE, SIDE, 2) + w_out.shape, BF),
            wide, wide, parts, square, sums, sums, blocks, blocks, blocks, blocks,
            pltpu.SemaphoreType.DMA((8,)),
            pltpu.SemaphoreType.DMA((1,)),
            ring, ring, pair, pair,
        ],
        compiler_params=pltpu.CompilerParams(
            collective_id=0, has_side_effects=True, vmem_limit_bytes=60 * 1024 * 1024
        ),
        name="layer",
    )(x, b, c, steps, cot, w_out)
    return tuple(r[None] for r in results)


def solution(mesh):
    tokens = P("dp", "ctx", None)
    return jax.shard_map(
        body,
        mesh=mesh,
        in_specs=(tokens, tokens, tokens, tokens, P(("dp", "ctx"), None), tokens),
        out_specs=(tokens, tokens, tokens, tokens),
        check_vma=False,
    )
```

```python
import functools

import jax
import jax.numpy as jnp
from jax import lax
from jax.experimental import pallas as pl
from jax.experimental.pallas import tpu as pltpu
from jax.sharding import PartitionSpec as P

decay_unit = 5e-05
rate = decay_unit * 1.4426950408889634
MESH = pl.DeviceIdType.MESH
F32 = jnp.float32
BF = jnp.bfloat16
LANES = 128
SIDE = 4
ORDERS = ((1, 0, 2), (0, 2, 1), (2, 1, 0))
CUTS = (0, 640, 1152, 2048)
WIDE = 2 * LANES
GROUP = 8


def dot(a, b):
    return lax.dot_general(a, b, (((1,), (0,)), ((), ())), preferred_element_type=F32)


def dot_nt(a, b):
    return lax.dot_general(a, b, (((1,), (1,)), ((), ())), preferred_element_type=F32)


def flip(a):
    return a.astype(F32).T


def span(j, size=LANES):
    return pl.ds(pl.multiple_of(j * size, size), size)


def grid_of(rows, columns):
    return (
        lax.broadcasted_iota(jnp.int32, (rows, columns), 0),
        lax.broadcasted_iota(jnp.int32, (rows, columns), 1),
    )


def greet_all(n):
    me, seq = lax.axis_index("ctx"), lax.axis_index("dp")
    barrier = pltpu.get_barrier_semaphore()

    def greet(i, carry):
        pl.semaphore_signal(
            barrier, inc=1, device_id={"ctx": lax.rem(me + i, n)}, device_id_type=MESH
        )
        return carry

    lax.fori_loop(1, n, greet, 0)
    for turn in (1, SIDE - 1):
        pl.semaphore_signal(
            barrier, inc=1, device_id={"dp": lax.rem(seq + turn, SIDE)}, device_id_type=MESH
        )
    return barrier


def copy_to(peer, source, target, sems, first):
    return pltpu.make_async_remote_copy(
        src_ref=source,
        dst_ref=target,
        send_sem=sems.at[first],
        recv_sem=sems.at[first + 1],
        device_id={"ctx": peer},
        device_id_type=MESH,
    )


def finish(n, source, target, sems, first):
    peer = lax.rem(lax.axis_index("ctx") + 1, n)
    some = pl.ds(0, n - 1)
    copy_to(peer, source.at[some], target.at[some], sems, first).wait()


def accumulate_decay(steps_t, level_t):
    heads, rows = steps_t.shape
    row, column = grid_of(rows, rows)
    ones = jnp.where(row <= column, 1.0, 0.0).astype(BF)
    value = steps_t[...]
    high = (value >> 7).astype(F32).astype(BF)
    low = (value & 127).astype(F32).astype(BF)
    level_t[...] = jnp.zeros_like(level_t)
    level_t[:heads, :] = (dot(high, ones) * 128.0 + dot(low, ones)) * rate


def columns_of(level, q):
    rolled = pltpu.roll(level[...], lax.rem(LANES - 4 * q, LANES), 1)
    return [jnp.broadcast_to(rolled[:, i : i + 1], rolled.shape) for i in range(4)]


def spread(level, q):
    parts = columns_of(level, q)
    _, column = grid_of(*parts[0].shape)
    left = column < LANES // 2
    both = jnp.concatenate(
        [jnp.where(left, parts[0], parts[1]), jnp.where(left, parts[2], parts[3])], axis=1
    )
    return both, both[both.shape[0] - 1 :]


def beside(blocks, q):
    return jnp.concatenate([blocks[2 * q], blocks[2 * q + 1]], axis=1)


def split_heads(value):
    _, column = grid_of(*value.shape)
    wide = value.astype(F32)
    left = jnp.where(column < LANES // 2, wide, 0.0).astype(BF)
    right = jnp.where(column < LANES // 2, 0.0, wide).astype(BF)
    return jnp.concatenate([left, right], axis=0)


class Gather:
    def __init__(self, shard, whole, own_sem, ring_send, ring_recv, pair_send, pair_recv):
        ctx = lax.axis_index("ctx")
        self.at = (lax.axis_index("dp"), ctx // (2 * SIDE), lax.rem(ctx // 2, SIDE))
        self.core = lax.rem(ctx, 2)
        self.shard, self.whole = shard, whole
        self.own_sem = own_sem
        self.ring_send, self.ring_recv = ring_send, ring_recv
        self.pair_send, self.pair_recv = pair_send, pair_recv

    def device(self, dim, place, core):
        y, x, z = [place if d == dim else v for d, v in enumerate(self.at)]
        return {"dp": y, "ctx": (x * SIDE + z) * 2 + core}

    def region(self, part, phase, place, rows):
        order = ORDERS[part]
        index = list(self.at)
        for dim in order[:phase]:
            index[dim] = slice(None)
        index[order[phase]] = place
        columns = pl.ds(CUTS[part], CUTS[part + 1] - CUTS[part])
        return self.whole.at[(*index, self.core, rows, columns)]

    def ring(self, part, phase, step):
        dim = ORDERS[part][phase]
        here = self.at[dim]
        right, left = lax.rem(here + 1, SIDE), lax.rem(here + SIDE - 1, SIDE)
        rows = self.shard.shape[0]
        for side, (peer, other) in enumerate(((right, left), (left, right))):
            if step == 0:
                piece = self.region(part, phase, here, pl.ds(0, rows))
            else:
                piece = self.region(part, phase, other, pl.ds(side * (rows // 2), rows // 2))
            yield pltpu.make_async_remote_copy(
                src_ref=piece,
                dst_ref=piece,
                send_sem=self.ring_send.at[part, phase, step, side],
                recv_sem=self.ring_recv.at[part, phase, step, side],
                device_id=self.device(dim, peer, self.core),
                device_id_type=MESH,
            )

    def pair(self, part, turn):
        dim = ORDERS[part][2]
        place = lax.rem(self.at[dim] + turn, SIDE)
        piece = self.region(part, 2, place, pl.ds(0, self.shard.shape[0]))
        return pltpu.make_async_remote_copy(
            src_ref=piece,
            dst_ref=piece,
            send_sem=self.pair_send.at[part, turn],
            recv_sem=self.pair_recv.at[part, turn],
            device_id=self.device(None, None, 1 - self.core),
            device_id_type=MESH,
        )

    def post(self, part, number):
        for copy in self.ring(part, number // 2, number % 2):
            copy.start()

    def begin(self):
        own = pltpu.make_async_copy(
            self.shard, self.whole.at[(*self.at, self.core)], self.own_sem.at[0]
        )
        own.start()
        own.wait()
        for part in range(3):
            self.post(part, 0)

    def advance(self, number):
        turns = {3: (0,), 4: (1, 3), 5: (2,)}.get(number, ())
        for part in range(3):
            for copy in self.ring(part, number // 2, number % 2):
                copy.wait()
            if number < 5:
                self.post(part, number + 1)
            for turn in turns:
                self.pair(part, turn).start()

    def end(self):
        for part in range(3):
            for turn in range(SIDE):
                self.pair(part, turn).wait()


def layer_kernel(
    n, scale, x, b, c, steps_t, cot, shard, out, grad_x, grad_b, grad_c,
    level, level_t, masked, masked_t, b_t, c_t, decays, y, send, recv, stage, before, mixed,
    whole, back, dshift, flow, inner_sum, b_sum, c_sum, send2, recv2, stage2, after, falls, tails, shifts,
    sems, own_sem, ring_send, ring_recv, pair_send, pair_recv,
):
    me = lax.axis_index("ctx")
    rows = x.shape[0]
    state = b.shape[1]
    barrier = greet_all(n)
    gather = Gather(shard, whole, own_sem, ring_send, ring_recv, pair_send, pair_recv)
    pl.semaphore_wait(barrier, n + 1)
    gather.begin()

    accumulate_decay(steps_t, level_t)
    level[...] = flip(level_t[...])
    row, column = grid_of(rows, rows)
    masked[...] = jnp.where(row >= column, scale * dot_nt(c[...], b[...]), 0.0)
    masked_t[...] = jnp.where(row <= column, scale * dot_nt(b[...], c[...]), 0.0)
    b_t[...] = flip(b[...]).astype(BF)
    c_t[...] = flip(c[...]).astype(BF)
    inner_sum[...] = jnp.zeros_like(inner_sum)
    b_sum[...] = jnp.zeros_like(b_sum)
    c_sum[...] = jnp.zeros_like(c_sum)

    def make_term(q, carry):
        both, last = spread(level, q)
        falls[q] = jnp.exp2(-both)
        tail = jnp.exp2(both - last)
        tails[q] = tail
        shifted = (x[:, span(q, WIDE)].astype(F32) * tail).astype(BF)
        shifts[:, span(q, WIDE)] = shifted
        term = dot(b_t[...], shifted).astype(BF)
        d = jnp.exp2(-last)
        high = d.astype(BF).astype(F32)
        middle = (d - high).astype(BF).astype(F32)
        low = d - high - middle
        which, _ = grid_of(16, WIDE)
        parts = jnp.where(which == 0, high, jnp.where(which == 1, middle, low))
        parts = jnp.where(which < 3, parts, 0.0).astype(BF)
        for u in range(2):
            send[2 * q + u, :state] = term[:, u * LANES : (u + 1) * LANES]
            send[2 * q + u, state:] = parts[:, u * LANES : (u + 1) * LANES]
        return carry

    def inside(q, carry):
        columns = columns_of(level, q)
        for u in range(2):
            mix = []
            for v in (2 * u, 2 * u + 1):
                gap = level_t[pl.ds(4 * q + v, 1), :] - columns[v]
                mix.append((masked[...] * jnp.exp2(jnp.minimum(gap, 0.0))).astype(BF))
            y[2 * q + u] = dot(jnp.concatenate(mix, axis=1), split_heads(x[:, span(2 * q + u)]))
        return carry

    gather.advance(0)
    lax.fori_loop(0, n // 8, make_term, 0)
    gather.advance(1)
    lax.fori_loop(n // 8, n // 2, make_term, 0)
    gather.advance(2)
    lax.fori_loop(0, n // 8, inside, 0)
    gather.advance(3)

    def post_term(i, carry):
        j = lax.rem(me + i, n)
        copy_to(j, send.at[j], recv.at[me], sems, 0).start()
        return carry

    lax.fori_loop(1, n, post_term, 0)
    recv[me] = send[me]
    lax.fori_loop(n // 8, n // 2, inside, 0)
    gather.advance(4)
    finish(n, send, recv, sems, 0)

    def step(g, carry):
        for u in range(GROUP):
            k = g * GROUP + u
            stage[k] = carry.astype(BF)
            parts = recv[k, state:].astype(F32)
            d = parts[0:1] + parts[1:2] + parts[2:3]
            decays[k] = jnp.broadcast_to(d, (8, LANES))
            carry = d * carry + recv[k, :state].astype(F32)

        def post(k, nothing):
            @pl.when(k != me)
            def _():
                copy_to(k, stage.at[k], before.at[me], sems, 2).start()

            return nothing

        lax.fori_loop(g * GROUP, (g + 1) * GROUP, post, 0)
        return carry

    lax.fori_loop(0, n // GROUP, step, jnp.zeros((state, LANES), F32))
    before[me] = stage[me]
    gather.advance(5)
    gather.end()

    def place(i):
        return lax.rem(me // 2 + 1 + i, n // 2)

    def make_back(i):
        q = place(i)
        chunk = whole[q // SIDE, lax.rem(q, SIDE)].reshape(WIDE, cot.shape[1])
        back[:, span(q, WIDE)] = dot_nt(cot[...], chunk).astype(BF)

    def make_term_back(i):
        q = place(i)
        shift = (back[:, span(q, WIDE)].astype(F32) * falls[q]).astype(BF)
        dshift[:, span(q, WIDE)] = shift
        term = dot(c_t[...], shift).astype(BF)
        for u in range(2):
            send2[2 * q + u] = term[:, u * LANES : (u + 1) * LANES]

    def post_back(i):
        for u in range(2):
            j = place(i) * 2 + u

            @pl.when(j != me)
            def _():
                copy_to(j, send2.at[j], recv2.at[me], sems, 4).start()

    def send_term(i, carry):
        make_term_back(i - 1)
        make_back(i)
        post_back(i - 1)
        return carry

    make_back(0)
    lax.fori_loop(1, n // 2, send_term, 0)
    make_term_back(n // 2 - 1)
    post_back(n // 2 - 1)
    recv2[me] = send2[me]
    finish(n, stage, before, sems, 2)

    def inside_back(q, carry):
        columns = columns_of(level, q)
        total = inner_sum[...]
        for u in range(2):
            j = 2 * q + u
            part = back[:, span(j)]
            pair = dot_nt(split_heads(x[:, span(j)]), part)
            mix = []
            for v in range(2):
                gap = columns[2 * u + v] - level_t[pl.ds(4 * q + 2 * u + v, 1), :]
                fade = jnp.exp2(jnp.minimum(gap, 0.0))
                mix.append((masked_t[...] * fade).astype(BF))
                total = total + fade * pair[v * rows : (v + 1) * rows]
            flow[j] = dot(jnp.concatenate(mix, axis=1), split_heads(part))
        inner_sum[...] = total
        c_sum[...] += dot_nt(dshift[:, span(q, WIDE)], beside(before, q))
        return carry

    lax.fori_loop(0, n // 2, inside_back, 0)
    finish(n, send2, recv2, sems, 4)

    def step_back(g, carry):
        for u in range(GROUP):
            k = n - 1 - (g * GROUP + u)
            stage2[k] = carry.astype(BF)
            carry = decays[k, 0:1] * carry + recv2[k].astype(F32)

        def post(i, nothing):
            k = n - 1 - i

            @pl.when(k != me)
            def _():
                copy_to(k, stage2.at[k], after.at[me], sems, 6).start()

            return nothing

        lax.fori_loop(g * GROUP, (g + 1) * GROUP, post, 0)
        return carry

    lax.fori_loop(0, n // GROUP, step_back, jnp.zeros((state, LANES), F32))
    after[me] = stage2[me]

    def join(q, carry):
        carried = scale * falls[q] * dot(c[...], beside(before, q))
        mixed[:, span(q, WIDE)] = (beside(y, q) + carried).astype(BF)
        return carry

    lax.fori_loop(0, n // 2, join, 0)

    def project(i, carry):
        chunk = whole[:, :, :, :, :, span(i, 256)].reshape(x.shape[1], 256)
        out[:, span(i, 256)] = dot(mixed[...], chunk).astype(BF)
        return carry

    lax.fori_loop(0, out.shape[1] // 256, project, 0)
    kernel_t = jnp.where(row <= column, scale * inner_sum[...], 0.0)
    kernel = kernel_t.T.astype(BF)
    grad_c[...] = (dot(kernel, b[...]) + scale * c_sum[...]).astype(BF)
    finish(n, stage2, after, sems, 6)

    def join_back(q, carry):
        late = beside(after, q)
        carried = scale * tails[q] * dot(b[...], late)
        grad_x[:, span(q, WIDE)] = (beside(flow, q) + carried).astype(BF)
        b_sum[...] += dot_nt(shifts[:, span(q, WIDE)], late)
        return carry

    lax.fori_loop(0, n // 2, join_back, 0)
    grad_b[...] = (dot(kernel_t.astype(BF), c[...]) + scale * b_sum[...]).astype(BF)


def body(x_in, b_in, c_in, log_decay, w_out, cotangent):
    x, b, c, steps, cot = x_in[0], b_in[0], c_in[0], log_decay[0], cotangent[0]
    rows = x.shape[0]
    state = b.shape[1]
    n = lax.axis_size("ctx")
    scale = (state * rows * n) ** (-0.5)
    vmem = pl.BlockSpec(memory_space=pltpu.VMEM)
    shape = jax.ShapeDtypeStruct
    square = pltpu.VMEM((rows, rows), F32)
    turned = pltpu.VMEM((state, rows), BF)
    blocks = pltpu.VMEM((n, state, LANES), BF)
    marked = pltpu.VMEM((n, state + 16, LANES), BF)
    parts = pltpu.VMEM((n, rows, LANES), F32)
    wide = pltpu.VMEM(x.shape, BF)
    spreads = pltpu.VMEM((n // 2, rows, WIDE), F32)
    sums = pltpu.VMEM((rows, state), F32)
    ring = pltpu.SemaphoreType.DMA((3, 3, 2, 2))
    pair = pltpu.SemaphoreType.DMA((3, SIDE))
    results = pl.pallas_call(
        functools.partial(layer_kernel, n, scale),
        out_shape=(
            shape(cot.shape, BF), shape(x.shape, BF), shape(b.shape, BF), shape(c.shape, BF),
        ),
        in_specs=[vmem] * 6,
        out_specs=(vmem,) * 4,
        scratch_shapes=[
            square, square, square, square, turned, turned,
            pltpu.VMEM((n, 8, LANES), F32),
            parts, marked, marked, blocks, blocks, wide,
            pltpu.VMEM((SIDE, SIDE, SIDE, 2) + w_out.shape, BF),
            wide, wide, parts, square, sums, sums, blocks, blocks, blocks, blocks,
            spreads, spreads, wide,
            pltpu.SemaphoreType.DMA((8,)),
            pltpu.SemaphoreType.DMA((1,)),
            ring, ring, pair, pair,
        ],
        compiler_params=pltpu.CompilerParams(
            collective_id=0, has_side_effects=True, vmem_limit_bytes=60 * 1024 * 1024
        ),
        name="layer",
    )(x, b, c, steps.T, cot, w_out)
    return tuple(r[None] for r in results)


def solution(mesh):
    tokens = P("dp", "ctx", None)
    return jax.shard_map(
        body,
        mesh=mesh,
        in_specs=(tokens, tokens, tokens, tokens, P(("dp", "ctx"), None), tokens),
        out_specs=(tokens, tokens, tokens, tokens),
        check_vma=False,
    )
```

```python
import functools

import jax
import jax.numpy as jnp
from jax import lax
from jax.experimental import pallas as pl
from jax.experimental.pallas import tpu as pltpu
from jax.sharding import PartitionSpec as P

decay_unit = 5e-05
rate = decay_unit * 1.4426950408889634
MESH = pl.DeviceIdType.MESH
F32 = jnp.float32
BF = jnp.bfloat16
LANES = 128
SIDE = 4
ORDERS = ((1, 0, 2), (0, 2, 1), (2, 1, 0))
CUTS = (0, 512, 1024, 2048)
WIDE = 2 * LANES
GROUP = 8


def dot(a, b):
    return lax.dot_general(a, b, (((1,), (0,)), ((), ())), preferred_element_type=F32)


def dot_nt(a, b):
    return lax.dot_general(a, b, (((1,), (1,)), ((), ())), preferred_element_type=F32)


def flip(a):
    return a.astype(F32).T


def span(j, size=LANES):
    return pl.ds(pl.multiple_of(j * size, size), size)


def grid_of(rows, columns):
    return (
        lax.broadcasted_iota(jnp.int32, (rows, columns), 0),
        lax.broadcasted_iota(jnp.int32, (rows, columns), 1),
    )


def greet_all(n):
    me, seq = lax.axis_index("ctx"), lax.axis_index("dp")
    barrier = pltpu.get_barrier_semaphore()

    def greet(i, carry):
        pl.semaphore_signal(
            barrier, inc=1, device_id={"ctx": lax.rem(me + i, n)}, device_id_type=MESH
        )
        return carry

    lax.fori_loop(1, n, greet, 0)
    for turn in (1, SIDE - 1):
        pl.semaphore_signal(
            barrier, inc=1, device_id={"dp": lax.rem(seq + turn, SIDE)}, device_id_type=MESH
        )
    return barrier


def copy_to(peer, source, target, sems, first):
    return pltpu.make_async_remote_copy(
        src_ref=source,
        dst_ref=target,
        send_sem=sems.at[first],
        recv_sem=sems.at[first + 1],
        device_id={"ctx": peer},
        device_id_type=MESH,
    )


def finish(n, source, target, sems, first):
    peer = lax.rem(lax.axis_index("ctx") + 1, n)
    some = pl.ds(0, n - 1)
    copy_to(peer, source.at[some], target.at[some], sems, first).wait()


def accumulate_decay(steps_t, level_t):
    heads, rows = steps_t.shape
    row, column = grid_of(rows, rows)
    ones = jnp.where(row <= column, 1.0, 0.0).astype(BF)
    value = steps_t[...]
    high = (value >> 7).astype(F32).astype(BF)
    low = (value & 127).astype(F32).astype(BF)
    level_t[...] = jnp.zeros_like(level_t)
    level_t[:heads, :] = (dot(high, ones) * 128.0 + dot(low, ones)) * rate


def columns_of(level, q):
    rolled = pltpu.roll(level[...], lax.rem(LANES - 4 * q, LANES), 1)
    return [jnp.broadcast_to(rolled[:, i : i + 1], rolled.shape) for i in range(4)]


def spread(level, q):
    parts = columns_of(level, q)
    _, column = grid_of(*parts[0].shape)
    left = column < LANES // 2
    both = jnp.concatenate(
        [jnp.where(left, parts[0], parts[1]), jnp.where(left, parts[2], parts[3])], axis=1
    )
    return both, both[both.shape[0] - 1 :]


def beside(blocks, q):
    return jnp.concatenate([blocks[2 * q], blocks[2 * q + 1]], axis=1)


def split_heads(value):
    _, column = grid_of(*value.shape)
    wide = value.astype(F32)
    left = jnp.where(column < LANES // 2, wide, 0.0).astype(BF)
    right = jnp.where(column < LANES // 2, 0.0, wide).astype(BF)
    return jnp.concatenate([left, right], axis=0)


class Gather:
    def __init__(self, shard, whole, own_sem, ring_send, ring_recv, pair_send, pair_recv):
        ctx = lax.axis_index("ctx")
        self.at = (lax.axis_index("dp"), ctx // (2 * SIDE), lax.rem(ctx // 2, SIDE))
        self.core = lax.rem(ctx, 2)
        self.shard, self.whole = shard, whole
        self.own_sem = own_sem
        self.ring_send, self.ring_recv = ring_send, ring_recv
        self.pair_send, self.pair_recv = pair_send, pair_recv

    def device(self, dim, place, core):
        y, x, z = [place if d == dim else v for d, v in enumerate(self.at)]
        return {"dp": y, "ctx": (x * SIDE + z) * 2 + core}

    def region(self, part, phase, place, rows):
        order = ORDERS[part]
        index = list(self.at)
        for dim in order[:phase]:
            index[dim] = slice(None)
        index[order[phase]] = place
        columns = pl.ds(CUTS[part], CUTS[part + 1] - CUTS[part])
        return self.whole.at[(*index, self.core, rows, columns)]

    def ring(self, part, phase, step):
        dim = ORDERS[part][phase]
        here = self.at[dim]
        right, left = lax.rem(here + 1, SIDE), lax.rem(here + SIDE - 1, SIDE)
        rows = self.shard.shape[0]
        for side, (peer, other) in enumerate(((right, left), (left, right))):
            if step == 0:
                piece = self.region(part, phase, here, pl.ds(0, rows))
            else:
                piece = self.region(part, phase, other, pl.ds(side * (rows // 2), rows // 2))
            yield pltpu.make_async_remote_copy(
                src_ref=piece,
                dst_ref=piece,
                send_sem=self.ring_send.at[part, phase, step, side],
                recv_sem=self.ring_recv.at[part, phase, step, side],
                device_id=self.device(dim, peer, self.core),
                device_id_type=MESH,
            )

    def pair(self, part, turn):
        dim = ORDERS[part][2]
        place = lax.rem(self.at[dim] + turn, SIDE)
        piece = self.region(part, 2, place, pl.ds(0, self.shard.shape[0]))
        return pltpu.make_async_remote_copy(
            src_ref=piece,
            dst_ref=piece,
            send_sem=self.pair_send.at[part, turn],
            recv_sem=self.pair_recv.at[part, turn],
            device_id=self.device(None, None, 1 - self.core),
            device_id_type=MESH,
        )

    def post(self, part, number):
        for copy in self.ring(part, number // 2, number % 2):
            copy.start()

    def begin(self):
        own = pltpu.make_async_copy(
            self.shard, self.whole.at[(*self.at, self.core)], self.own_sem.at[0]
        )
        own.start()
        own.wait()
        for part in range(3):
            self.post(part, 0)

    def advance(self, number, parts=(0, 1, 2)):
        turns = {3: (0,), 4: (1, 3), 5: (2,)}.get(number, ())
        for part in parts:
            for copy in self.ring(part, number // 2, number % 2):
                copy.wait()
            if number < 5:
                self.post(part, number + 1)
            for turn in turns:
                self.pair(part, turn).start()

    def end(self, parts):
        for part in parts:
            for turn in range(SIDE):
                self.pair(part, turn).wait()


def layer_kernel(
    n, scale, x, b, c, steps_t, cot, shard, out, grad_x, grad_b, grad_c,
    level, level_t, masked, masked_t, b_t, c_t, decays, y, send, recv, stage, before, mixed,
    whole, back, dshift, flow, inner_sum, b_sum, c_sum, send2, recv2, stage2, after, falls, tails, shifts,
    sems, own_sem, ring_send, ring_recv, pair_send, pair_recv,
):
    me = lax.axis_index("ctx")
    rows = x.shape[0]
    state = b.shape[1]
    barrier = greet_all(n)
    gather = Gather(shard, whole, own_sem, ring_send, ring_recv, pair_send, pair_recv)
    pl.semaphore_wait(barrier, n + 1)
    gather.begin()

    accumulate_decay(steps_t, level_t)
    level[...] = flip(level_t[...])
    row, column = grid_of(rows, rows)
    masked[...] = jnp.where(row >= column, scale * dot_nt(c[...], b[...]), 0.0)
    masked_t[...] = jnp.where(row <= column, scale * dot_nt(b[...], c[...]), 0.0)
    b_t[...] = flip(b[...]).astype(BF)
    c_t[...] = flip(c[...]).astype(BF)
    inner_sum[...] = jnp.zeros_like(inner_sum)
    b_sum[...] = jnp.zeros_like(b_sum)
    c_sum[...] = jnp.zeros_like(c_sum)

    def make_term(q, carry):
        both, last = spread(level, q)
        falls[q] = jnp.exp2(-both)
        tail = jnp.exp2(both - last)
        tails[q] = tail
        shifted = (x[:, span(q, WIDE)].astype(F32) * tail).astype(BF)
        shifts[:, span(q, WIDE)] = shifted
        term = dot(b_t[...], shifted).astype(BF)
        d = jnp.exp2(-last)
        high = d.astype(BF).astype(F32)
        middle = (d - high).astype(BF).astype(F32)
        low = d - high - middle
        which, _ = grid_of(16, WIDE)
        parts = jnp.where(which == 0, high, jnp.where(which == 1, middle, low))
        parts = jnp.where(which < 3, parts, 0.0).astype(BF)
        for u in range(2):
            send[2 * q + u, :state] = term[:, u * LANES : (u + 1) * LANES]
            send[2 * q + u, state:] = parts[:, u * LANES : (u + 1) * LANES]
        return carry

    def inside(q, carry):
        columns = columns_of(level, q)
        for u in range(2):
            mix = []
            for v in (2 * u, 2 * u + 1):
                gap = level_t[pl.ds(4 * q + v, 1), :] - columns[v]
                mix.append((masked[...] * jnp.exp2(jnp.minimum(gap, 0.0))).astype(BF))
            y[2 * q + u] = dot(jnp.concatenate(mix, axis=1), split_heads(x[:, span(2 * q + u)]))
        return carry

    gather.advance(0)
    lax.fori_loop(0, n // 8, make_term, 0)
    gather.advance(1)
    lax.fori_loop(n // 8, n // 2, make_term, 0)
    gather.advance(2)
    lax.fori_loop(0, n // 8, inside, 0)
    gather.advance(3)

    def post_term(i, carry):
        j = lax.rem(me + i, n)
        copy_to(j, send.at[j], recv.at[me], sems, 0).start()
        return carry

    lax.fori_loop(1, n, post_term, 0)
    recv[me] = send[me]
    lax.fori_loop(n // 8, n // 2, inside, 0)
    gather.advance(4)
    finish(n, send, recv, sems, 0)

    def step(g, carry):
        for u in range(GROUP):
            k = g * GROUP + u
            stage[k] = carry.astype(BF)
            parts = recv[k, state:].astype(F32)
            d = parts[0:1] + parts[1:2] + parts[2:3]
            decays[k] = jnp.broadcast_to(d, (8, LANES))
            carry = d * carry + recv[k, :state].astype(F32)

        def post(k, nothing):
            @pl.when(k != me)
            def _():
                copy_to(k, stage.at[k], before.at[me], sems, 2).start()

            return nothing

        lax.fori_loop(g * GROUP, (g + 1) * GROUP, post, 0)
        return carry

    lax.fori_loop(0, n // GROUP, step, jnp.zeros((state, LANES), F32))
    before[me] = stage[me]
    gather.advance(5, (0, 1))
    gather.end((0, 1))

    def place(i):
        return lax.rem(me // 2 + 1 + i, n // 2)

    early, late = pl.ds(0, CUTS[2]), pl.ds(CUTS[2], CUTS[3] - CUTS[2])

    def share(q, columns):
        chunk = whole[q // SIDE, lax.rem(q, SIDE), :, :, :, columns]
        return dot_nt(cot[:, columns], chunk.reshape(WIDE, chunk.shape[-1]))

    def begin_back(q, carry):
        part = share(q, early)
        for u in range(2):
            flow[2 * q + u] = part[:, u * LANES : (u + 1) * LANES]
        return carry

    lax.fori_loop(0, n // 2, begin_back, 0)
    gather.advance(5, (2,))
    gather.end((2,))

    def make_back(i):
        q = place(i)
        back[:, span(q, WIDE)] = (beside(flow, q) + share(q, late)).astype(BF)

    def make_term_back(i):
        q = place(i)
        shift = (back[:, span(q, WIDE)].astype(F32) * falls[q]).astype(BF)
        dshift[:, span(q, WIDE)] = shift
        term = dot(c_t[...], shift).astype(BF)
        for u in range(2):
            send2[2 * q + u] = term[:, u * LANES : (u + 1) * LANES]

    def post_back(i):
        for u in range(2):
            j = place(i) * 2 + u

            @pl.when(j != me)
            def _():
                copy_to(j, send2.at[j], recv2.at[me], sems, 4).start()

    def send_term(i, carry):
        make_term_back(i - 1)
        make_back(i)
        post_back(i - 1)
        return carry

    make_back(0)
    lax.fori_loop(1, n // 2, send_term, 0)
    make_term_back(n // 2 - 1)
    post_back(n // 2 - 1)
    recv2[me] = send2[me]
    finish(n, stage, before, sems, 2)

    def inside_back(q, carry):
        columns = columns_of(level, q)
        total = inner_sum[...]
        for u in range(2):
            j = 2 * q + u
            part = back[:, span(j)]
            pair = dot_nt(split_heads(x[:, span(j)]), part)
            mix = []
            for v in range(2):
                gap = columns[2 * u + v] - level_t[pl.ds(4 * q + 2 * u + v, 1), :]
                fade = jnp.exp2(jnp.minimum(gap, 0.0))
                mix.append((masked_t[...] * fade).astype(BF))
                total = total + fade * pair[v * rows : (v + 1) * rows]
            flow[j] = dot(jnp.concatenate(mix, axis=1), split_heads(part))
        inner_sum[...] = total
        c_sum[...] += dot_nt(dshift[:, span(q, WIDE)], beside(before, q))
        return carry

    lax.fori_loop(0, n // 2, inside_back, 0)
    finish(n, send2, recv2, sems, 4)

    def step_back(g, carry):
        for u in range(GROUP):
            k = n - 1 - (g * GROUP + u)
            stage2[k] = carry.astype(BF)
            carry = decays[k, 0:1] * carry + recv2[k].astype(F32)

        def post(i, nothing):
            k = n - 1 - i

            @pl.when(k != me)
            def _():
                copy_to(k, stage2.at[k], after.at[me], sems, 6).start()

            return nothing

        lax.fori_loop(g * GROUP, (g + 1) * GROUP, post, 0)
        return carry

    lax.fori_loop(0, n // GROUP, step_back, jnp.zeros((state, LANES), F32))
    after[me] = stage2[me]

    def join(q, carry):
        carried = scale * falls[q] * dot(c[...], beside(before, q))
        mixed[:, span(q, WIDE)] = (beside(y, q) + carried).astype(BF)
        return carry

    lax.fori_loop(0, n // 2, join, 0)

    def project(i, carry):
        chunk = whole[:, :, :, :, :, span(i, 256)].reshape(x.shape[1], 256)
        out[:, span(i, 256)] = dot(mixed[...], chunk).astype(BF)
        return carry

    lax.fori_loop(0, out.shape[1] // 256, project, 0)
    kernel_t = jnp.where(row <= column, scale * inner_sum[...], 0.0)
    kernel = kernel_t.T.astype(BF)
    grad_c[...] = (dot(kernel, b[...]) + scale * c_sum[...]).astype(BF)
    finish(n, stage2, after, sems, 6)

    def join_back(q, carry):
        late = beside(after, q)
        carried = scale * tails[q] * dot(b[...], late)
        grad_x[:, span(q, WIDE)] = (beside(flow, q) + carried).astype(BF)
        b_sum[...] += dot_nt(shifts[:, span(q, WIDE)], late)
        return carry

    lax.fori_loop(0, n // 2, join_back, 0)
    grad_b[...] = (dot(kernel_t.astype(BF), c[...]) + scale * b_sum[...]).astype(BF)


def body(x_in, b_in, c_in, log_decay, w_out, cotangent):
    x, b, c, steps, cot = x_in[0], b_in[0], c_in[0], log_decay[0], cotangent[0]
    rows = x.shape[0]
    state = b.shape[1]
    n = lax.axis_size("ctx")
    scale = (state * rows * n) ** (-0.5)
    vmem = pl.BlockSpec(memory_space=pltpu.VMEM)
    shape = jax.ShapeDtypeStruct
    square = pltpu.VMEM((rows, rows), F32)
    turned = pltpu.VMEM((state, rows), BF)
    blocks = pltpu.VMEM((n, state, LANES), BF)
    marked = pltpu.VMEM((n, state + 16, LANES), BF)
    parts = pltpu.VMEM((n, rows, LANES), F32)
    wide = pltpu.VMEM(x.shape, BF)
    spreads = pltpu.VMEM((n // 2, rows, WIDE), F32)
    sums = pltpu.VMEM((rows, state), F32)
    ring = pltpu.SemaphoreType.DMA((3, 3, 2, 2))
    pair = pltpu.SemaphoreType.DMA((3, SIDE))
    results = pl.pallas_call(
        functools.partial(layer_kernel, n, scale),
        out_shape=(
            shape(cot.shape, BF), shape(x.shape, BF), shape(b.shape, BF), shape(c.shape, BF),
        ),
        in_specs=[vmem] * 6,
        out_specs=(vmem,) * 4,
        scratch_shapes=[
            square, square, square, square, turned, turned,
            pltpu.VMEM((n, 8, LANES), F32),
            parts, marked, marked, blocks, blocks, wide,
            pltpu.VMEM((SIDE, SIDE, SIDE, 2) + w_out.shape, BF),
            wide, wide, parts, square, sums, sums, blocks, blocks, blocks, blocks,
            spreads, spreads, wide,
            pltpu.SemaphoreType.DMA((8,)),
            pltpu.SemaphoreType.DMA((1,)),
            ring, ring, pair, pair,
        ],
        compiler_params=pltpu.CompilerParams(
            collective_id=0, has_side_effects=True, vmem_limit_bytes=60 * 1024 * 1024
        ),
        name="layer",
    )(x, b, c, steps.T, cot, w_out)
    return tuple(r[None] for r in results)


def solution(mesh):
    tokens = P("dp", "ctx", None)
    return jax.shard_map(
        body,
        mesh=mesh,
        in_specs=(tokens, tokens, tokens, tokens, P(("dp", "ctx"), None), tokens),
        out_specs=(tokens, tokens, tokens, tokens),
        check_vma=False,
    )
```

```python
import functools

import jax
import jax.numpy as jnp
from jax import lax
from jax.experimental import pallas as pl
from jax.experimental.pallas import tpu as pltpu
from jax.sharding import PartitionSpec as P

decay_unit = 5e-05
rate = decay_unit * 1.4426950408889634
MESH = pl.DeviceIdType.MESH
F32 = jnp.float32
BF = jnp.bfloat16
LANES = 128
SIDE = 4
ORDERS = ((1, 0, 2), (0, 2, 1), (2, 1, 0))
CUTS = (0, 512, 1024, 2048)
WIDE = 2 * LANES
GROUP = 8


def dot(a, b):
    return lax.dot_general(a, b, (((1,), (0,)), ((), ())), preferred_element_type=F32)


def dot_nt(a, b):
    return lax.dot_general(a, b, (((1,), (1,)), ((), ())), preferred_element_type=F32)


def flip(a):
    return a.astype(F32).T


def span(j, size=LANES):
    return pl.ds(pl.multiple_of(j * size, size), size)


def grid_of(rows, columns):
    return (
        lax.broadcasted_iota(jnp.int32, (rows, columns), 0),
        lax.broadcasted_iota(jnp.int32, (rows, columns), 1),
    )


def greet_all(n):
    me, seq = lax.axis_index("ctx"), lax.axis_index("dp")
    barrier = pltpu.get_barrier_semaphore()

    def greet(i, carry):
        pl.semaphore_signal(
            barrier, inc=1, device_id={"ctx": lax.rem(me + 2 * i, n)}, device_id_type=MESH
        )
        return carry

    lax.fori_loop(1, n // 2, greet, 0)
    pl.semaphore_signal(
        barrier, inc=1, device_id={"ctx": me + 1 - 2 * lax.rem(me, 2)}, device_id_type=MESH
    )
    for turn in (1, SIDE - 1):
        pl.semaphore_signal(
            barrier, inc=1, device_id={"dp": lax.rem(seq + turn, SIDE)}, device_id_type=MESH
        )
    return barrier


def copy_to(peer, source, target, sems, first):
    return pltpu.make_async_remote_copy(
        src_ref=source,
        dst_ref=target,
        send_sem=sems.at[first],
        recv_sem=sems.at[first + 1],
        device_id={"ctx": peer},
        device_id_type=MESH,
    )


def finish(n, source, target, sems, first):
    peer = lax.rem(lax.axis_index("ctx") + 2, n)
    some = pl.ds(0, n // 2 - 1)
    copy_to(peer, source.at[some], target.at[some], sems, first).wait()


def in_parts(d):
    high = d.astype(BF).astype(F32)
    middle = (d - high).astype(BF).astype(F32)
    low = d - high - middle
    which, _ = grid_of(16, d.shape[1])
    parts = jnp.where(which == 0, high, jnp.where(which == 1, middle, low))
    return jnp.where(which < 3, parts, 0.0).astype(BF)


def from_parts(rows):
    parts = rows.astype(F32)
    return parts[0:1] + parts[1:2] + parts[2:3]


def accumulate_decay(steps_t, level_t):
    heads, rows = steps_t.shape
    row, column = grid_of(rows, rows)
    ones = jnp.where(row <= column, 1.0, 0.0).astype(BF)
    value = steps_t[...]
    high = (value >> 7).astype(F32).astype(BF)
    low = (value & 127).astype(F32).astype(BF)
    level_t[...] = jnp.zeros_like(level_t)
    level_t[:heads, :] = (dot(high, ones) * 128.0 + dot(low, ones)) * rate


def columns_of(level, q):
    rolled = pltpu.roll(level[...], lax.rem(LANES - 4 * q, LANES), 1)
    return [jnp.broadcast_to(rolled[:, i : i + 1], rolled.shape) for i in range(4)]


def spread(level, q):
    parts = columns_of(level, q)
    _, column = grid_of(*parts[0].shape)
    left = column < LANES // 2
    both = jnp.concatenate(
        [jnp.where(left, parts[0], parts[1]), jnp.where(left, parts[2], parts[3])], axis=1
    )
    return both, both[both.shape[0] - 1 :]


def beside(blocks, q):
    return jnp.concatenate([blocks[2 * q], blocks[2 * q + 1]], axis=1)


def both_of(slabs, q):
    return jnp.concatenate([slabs[0, q], slabs[1, q]], axis=1)


def split_heads(value):
    _, column = grid_of(*value.shape)
    wide = value.astype(F32)
    left = jnp.where(column < LANES // 2, wide, 0.0).astype(BF)
    right = jnp.where(column < LANES // 2, 0.0, wide).astype(BF)
    return jnp.concatenate([left, right], axis=0)


class Gather:
    def __init__(self, shard, whole, own_sem, ring_send, ring_recv, pair_send, pair_recv):
        ctx = lax.axis_index("ctx")
        self.at = (lax.axis_index("dp"), ctx // (2 * SIDE), lax.rem(ctx // 2, SIDE))
        self.core = lax.rem(ctx, 2)
        self.shard, self.whole = shard, whole
        self.own_sem = own_sem
        self.ring_send, self.ring_recv = ring_send, ring_recv
        self.pair_send, self.pair_recv = pair_send, pair_recv

    def device(self, dim, place, core):
        y, x, z = [place if d == dim else v for d, v in enumerate(self.at)]
        return {"dp": y, "ctx": (x * SIDE + z) * 2 + core}

    def region(self, part, phase, place, rows):
        order = ORDERS[part]
        index = list(self.at)
        for dim in order[:phase]:
            index[dim] = slice(None)
        index[order[phase]] = place
        columns = pl.ds(CUTS[part], CUTS[part + 1] - CUTS[part])
        return self.whole.at[(*index, self.core, rows, columns)]

    def ring(self, part, phase, step):
        dim = ORDERS[part][phase]
        here = self.at[dim]
        right, left = lax.rem(here + 1, SIDE), lax.rem(here + SIDE - 1, SIDE)
        rows = self.shard.shape[0]
        for side, (peer, other) in enumerate(((right, left), (left, right))):
            if step == 0:
                piece = self.region(part, phase, here, pl.ds(0, rows))
            else:
                piece = self.region(part, phase, other, pl.ds(side * (rows // 2), rows // 2))
            yield pltpu.make_async_remote_copy(
                src_ref=piece,
                dst_ref=piece,
                send_sem=self.ring_send.at[part, phase, step, side],
                recv_sem=self.ring_recv.at[part, phase, step, side],
                device_id=self.device(dim, peer, self.core),
                device_id_type=MESH,
            )

    def pair(self, part, turn):
        dim = ORDERS[part][2]
        place = lax.rem(self.at[dim] + turn, SIDE)
        piece = self.region(part, 2, place, pl.ds(0, self.shard.shape[0]))
        return pltpu.make_async_remote_copy(
            src_ref=piece,
            dst_ref=piece,
            send_sem=self.pair_send.at[part, turn],
            recv_sem=self.pair_recv.at[part, turn],
            device_id=self.device(None, None, 1 - self.core),
            device_id_type=MESH,
        )

    def post(self, part, number):
        for copy in self.ring(part, number // 2, number % 2):
            copy.start()

    def begin(self):
        own = pltpu.make_async_copy(
            self.shard, self.whole.at[(*self.at, self.core)], self.own_sem.at[0]
        )
        own.start()
        own.wait()
        for part in range(3):
            self.post(part, 0)

    def advance(self, number, parts=(0, 1, 2)):
        turns = {3: (0,), 4: (1, 3), 5: (2,)}.get(number, ())
        for part in parts:
            for copy in self.ring(part, number // 2, number % 2):
                copy.wait()
            if number < 5:
                self.post(part, number + 1)
            for turn in turns:
                self.pair(part, turn).start()

    def end(self, parts):
        for part in parts:
            for turn in range(SIDE):
                self.pair(part, turn).wait()


def layer_kernel(
    n, scale, x, b, c, steps_t, cot, shard, out, grad_x, grad_b, grad_c,
    level, level_t, masked, masked_t, b_t, c_t, decays, y, send, near, joint, recv, stage, got, give, before, mixed,
    whole, back, dshift, flow, inner_sum, b_sum, c_sum, send2, near2, joint2, recv2, stage2, got2, give2, after,
    falls, tails, shifts,
    sems, own_sem, ring_send, ring_recv, pair_send, pair_recv,
):
    me = lax.axis_index("ctx")
    rows = x.shape[0]
    state = b.shape[1]
    core, chip, chips = lax.rem(me, 2), me // 2, n // 2
    partner = me + 1 - 2 * core
    first = (1 - core).astype(F32)
    second = 1.0 - first
    barrier = greet_all(n)
    gather = Gather(shard, whole, own_sem, ring_send, ring_recv, pair_send, pair_recv)
    pl.semaphore_wait(barrier, n // 2 + 2)
    gather.begin()

    accumulate_decay(steps_t, level_t)
    level[...] = flip(level_t[...])
    row, column = grid_of(rows, rows)
    masked[...] = jnp.where(row >= column, scale * dot_nt(c[...], b[...]), 0.0)
    masked_t[...] = jnp.where(row <= column, scale * dot_nt(b[...], c[...]), 0.0)
    b_t[...] = flip(b[...]).astype(BF)
    c_t[...] = flip(c[...]).astype(BF)
    inner_sum[...] = jnp.zeros_like(inner_sum)
    b_sum[...] = jnp.zeros_like(b_sum)
    c_sum[...] = jnp.zeros_like(c_sum)

    def make_term(q, carry):
        both, last = spread(level, q)
        falls[q] = jnp.exp2(-both)
        tail = jnp.exp2(both - last)
        tails[q] = tail
        shifted = (x[:, span(q, WIDE)].astype(F32) * tail).astype(BF)
        shifts[:, span(q, WIDE)] = shifted
        term = dot(b_t[...], shifted).astype(BF)
        parts = in_parts(jnp.exp2(-last))
        for u in range(2):
            send[u, q, :state] = term[:, u * LANES : (u + 1) * LANES]
            send[u, q, state:] = parts[:, u * LANES : (u + 1) * LANES]
        return carry

    def inside(q, carry):
        columns = columns_of(level, q)
        for u in range(2):
            mix = []
            for v in (2 * u, 2 * u + 1):
                gap = level_t[pl.ds(4 * q + v, 1), :] - columns[v]
                mix.append((masked[...] * jnp.exp2(jnp.minimum(gap, 0.0))).astype(BF))
            y[2 * q + u] = dot(jnp.concatenate(mix, axis=1), split_heads(x[:, span(2 * q + u)]))
        return carry

    gather.advance(0)
    lax.fori_loop(0, n // 8, make_term, 0)
    gather.advance(1)
    lax.fori_loop(n // 8, n // 2, make_term, 0)
    near_terms = copy_to(partner, send.at[1 - core], near, sems, 0)
    near_terms.start()
    gather.advance(2)
    lax.fori_loop(0, n // 8, inside, 0)
    near_terms.wait()

    def combine(q, carry):
        mine, theirs = from_parts(send[core, q, state:]), from_parts(near[q, state:])
        here = (first * theirs + second) * send[core, q, :state].astype(F32)
        there = (second * mine + first) * near[q, :state].astype(F32)
        joint[q, :state] = (here + there).astype(BF)
        joint[q, state:] = in_parts(mine * theirs)
        return carry

    lax.fori_loop(0, chips, combine, 0)
    gather.advance(3)

    def post_term(i, carry):
        q = lax.rem(chip + i, chips)
        copy_to(2 * q + core, joint.at[q], recv.at[chip], sems, 2).start()
        return carry

    lax.fori_loop(1, chips, post_term, 0)
    recv[chip] = joint[chip]
    lax.fori_loop(n // 8, n // 2, inside, 0)
    gather.advance(4)
    finish(n, joint, recv, sems, 2)

    def step(g, carry):
        for u in range(GROUP):
            k = g * GROUP + u
            stage[k] = carry.astype(BF)
            d = from_parts(recv[k, state:])
            decays[k] = jnp.broadcast_to(d, (8, LANES))
            carry = d * carry + recv[k, :state].astype(F32)

        def post(k, nothing):
            @pl.when(k != chip)
            def _():
                copy_to(2 * k + core, stage.at[k], got.at[chip], sems, 4).start()

            return nothing

        lax.fori_loop(g * GROUP, (g + 1) * GROUP, post, 0)
        return carry

    lax.fori_loop(0, chips // GROUP, step, jnp.zeros((state, LANES), F32))
    got[chip] = stage[chip]
    gather.advance(5, (0, 1))
    gather.end((0, 1))

    def place(i):
        return lax.rem(me // 2 + 1 + i, n // 2)

    early, late = pl.ds(0, CUTS[2]), pl.ds(CUTS[2], CUTS[3] - CUTS[2])

    def share(q, columns):
        chunk = whole[q // SIDE, lax.rem(q, SIDE), :, :, :, columns]
        return dot_nt(cot[:, columns], chunk.reshape(WIDE, chunk.shape[-1]))

    def begin_back(q, carry):
        part = share(q, early)
        for u in range(2):
            flow[2 * q + u] = part[:, u * LANES : (u + 1) * LANES]
        return carry

    lax.fori_loop(0, n // 2, begin_back, 0)
    finish(n, stage, got, sems, 4)

    def pass_on(q, carry):
        early_state = got[q].astype(F32)
        d = first * from_parts(send[core, q, state:]) + second * from_parts(near[q, state:])
        term = first * send[core, q, :state].astype(F32) + second * near[q, :state].astype(F32)
        late_state = d * early_state + term
        before[core, q] = (first * early_state + second * late_state).astype(BF)
        give[q] = (first * late_state + second * early_state).astype(BF)
        return carry

    lax.fori_loop(0, chips, pass_on, 0)
    near_states = copy_to(partner, give, before.at[core], sems, 6)
    near_states.start()
    gather.advance(5, (2,))
    gather.end((2,))

    def make_back(i):
        q = place(i)
        back[:, span(q, WIDE)] = (beside(flow, q) + share(q, late)).astype(BF)

    def make_term_back(i):
        q = place(i)
        shift = (back[:, span(q, WIDE)].astype(F32) * falls[q]).astype(BF)
        dshift[:, span(q, WIDE)] = shift
        term = dot(c_t[...], shift).astype(BF)
        for u in range(2):
            send2[u, q] = term[:, u * LANES : (u + 1) * LANES]

    def post_back(i):
        q = place(i)
        copy_to(partner, send2.at[1 - core, q], near2.at[q], sems, 8).start()

    def send_term(i, carry):
        make_term_back(i - 1)
        make_back(i)
        post_back(i - 1)
        return carry

    make_back(0)
    lax.fori_loop(1, n // 2, send_term, 0)
    make_term_back(n // 2 - 1)
    post_back(n // 2 - 1)
    copy_to(partner, send2.at[1 - core], near2, sems, 8).wait()

    def combine_back(i, carry):
        q = lax.rem(chip + 1 + i, chips)
        mine, theirs = from_parts(send[core, q, state:]), from_parts(near[q, state:])
        here = (first + second * theirs) * send2[core, q].astype(F32)
        there = (first * mine + second) * near2[q].astype(F32)
        joint2[q] = (here + there).astype(BF)

        @pl.when(q != chip)
        def _():
            copy_to(2 * q + core, joint2.at[q], recv2.at[chip], sems, 10).start()

        return carry

    lax.fori_loop(0, chips, combine_back, 0)
    recv2[chip] = joint2[chip]
    near_states.wait()

    def inside_back(q, carry):
        columns = columns_of(level, q)
        total = inner_sum[...]
        for u in range(2):
            j = 2 * q + u
            part = back[:, span(j)]
            pair = dot_nt(split_heads(x[:, span(j)]), part)
            mix = []
            for v in range(2):
                gap = columns[2 * u + v] - level_t[pl.ds(4 * q + 2 * u + v, 1), :]
                fade = jnp.exp2(jnp.minimum(gap, 0.0))
                mix.append((masked_t[...] * fade).astype(BF))
                total = total + fade * pair[v * rows : (v + 1) * rows]
            flow[j] = dot(jnp.concatenate(mix, axis=1), split_heads(part))
        inner_sum[...] = total
        c_sum[...] += dot_nt(dshift[:, span(q, WIDE)], both_of(before, q))
        return carry

    lax.fori_loop(0, n // 2, inside_back, 0)
    finish(n, joint2, recv2, sems, 10)

    def step_back(g, carry):
        for u in range(GROUP):
            k = chips - 1 - (g * GROUP + u)
            stage2[k] = carry.astype(BF)
            carry = decays[k, 0:1] * carry + recv2[k].astype(F32)

        def post(i, nothing):
            k = chips - 1 - i

            @pl.when(k != chip)
            def _():
                copy_to(2 * k + core, stage2.at[k], got2.at[chip], sems, 12).start()

            return nothing

        lax.fori_loop(g * GROUP, (g + 1) * GROUP, post, 0)
        return carry

    lax.fori_loop(0, chips // GROUP, step_back, jnp.zeros((state, LANES), F32))
    got2[chip] = stage2[chip]

    def join(q, carry):
        carried = scale * falls[q] * dot(c[...], both_of(before, q))
        mixed[:, span(q, WIDE)] = (beside(y, q) + carried).astype(BF)
        return carry

    lax.fori_loop(0, n // 2, join, 0)

    finish(n, stage2, got2, sems, 12)

    def pass_back(q, carry):
        late_state = got2[q].astype(F32)
        d = first * from_parts(near[q, state:]) + second * from_parts(send[core, q, state:])
        term = first * near2[q].astype(F32) + second * send2[core, q].astype(F32)
        early_state = d * late_state + term
        after[core, q] = (first * early_state + second * late_state).astype(BF)
        give2[q] = (first * late_state + second * early_state).astype(BF)
        return carry

    lax.fori_loop(0, chips, pass_back, 0)
    near_after = copy_to(partner, give2, after.at[core], sems, 14)
    near_after.start()

    def project(i, carry):
        chunk = whole[:, :, :, :, :, span(i, 256)].reshape(x.shape[1], 256)
        out[:, span(i, 256)] = dot(mixed[...], chunk).astype(BF)
        return carry

    lax.fori_loop(0, out.shape[1] // 256, project, 0)
    kernel_t = jnp.where(row <= column, scale * inner_sum[...], 0.0)
    kernel = kernel_t.T.astype(BF)
    grad_c[...] = (dot(kernel, b[...]) + scale * c_sum[...]).astype(BF)
    near_after.wait()

    def join_back(q, carry):
        late = both_of(after, q)
        carried = scale * tails[q] * dot(b[...], late)
        grad_x[:, span(q, WIDE)] = (beside(flow, q) + carried).astype(BF)
        b_sum[...] += dot_nt(shifts[:, span(q, WIDE)], late)
        return carry

    lax.fori_loop(0, n // 2, join_back, 0)
    grad_b[...] = (dot(kernel_t.astype(BF), c[...]) + scale * b_sum[...]).astype(BF)


def body(x_in, b_in, c_in, log_decay, w_out, cotangent):
    x, b, c, steps, cot = x_in[0], b_in[0], c_in[0], log_decay[0], cotangent[0]
    rows = x.shape[0]
    state = b.shape[1]
    n = lax.axis_size("ctx")
    scale = (state * rows * n) ** (-0.5)
    vmem = pl.BlockSpec(memory_space=pltpu.VMEM)
    shape = jax.ShapeDtypeStruct
    square = pltpu.VMEM((rows, rows), F32)
    turned = pltpu.VMEM((state, rows), BF)
    blocks = pltpu.VMEM((n // 2, state, LANES), BF)
    marked = pltpu.VMEM((n // 2, state + 16, LANES), BF)
    slabs = pltpu.VMEM((2, n // 2, state, LANES), BF)
    marked_slabs = pltpu.VMEM((2, n // 2, state + 16, LANES), BF)
    parts = pltpu.VMEM((n, rows, LANES), F32)
    wide = pltpu.VMEM(x.shape, BF)
    spreads = pltpu.VMEM((n // 2, rows, WIDE), F32)
    sums = pltpu.VMEM((rows, state), F32)
    ring = pltpu.SemaphoreType.DMA((3, 3, 2, 2))
    pair = pltpu.SemaphoreType.DMA((3, SIDE))
    results = pl.pallas_call(
        functools.partial(layer_kernel, n, scale),
        out_shape=(
            shape(cot.shape, BF), shape(x.shape, BF), shape(b.shape, BF), shape(c.shape, BF),
        ),
        in_specs=[vmem] * 6,
        out_specs=(vmem,) * 4,
        scratch_shapes=[
            square, square, square, square, turned, turned,
            pltpu.VMEM((n // 2, 8, LANES), F32),
            parts, marked_slabs, marked, marked, marked, blocks, blocks, blocks, slabs, wide,
            pltpu.VMEM((SIDE, SIDE, SIDE, 2) + w_out.shape, BF),
            wide, wide, parts, square, sums, sums,
            slabs, blocks, blocks, blocks, blocks, blocks, blocks, slabs,
            spreads, spreads, wide,
            pltpu.SemaphoreType.DMA((16,)),
            pltpu.SemaphoreType.DMA((1,)),
            ring, ring, pair, pair,
        ],
        compiler_params=pltpu.CompilerParams(
            collective_id=0, has_side_effects=True, vmem_limit_bytes=60 * 1024 * 1024
        ),
        name="layer",
    )(x, b, c, steps.T, cot, w_out)
    return tuple(r[None] for r in results)


def solution(mesh):
    tokens = P("dp", "ctx", None)
    return jax.shard_map(
        body,
        mesh=mesh,
        in_specs=(tokens, tokens, tokens, tokens, P(("dp", "ctx"), None), tokens),
        out_specs=(tokens, tokens, tokens, tokens),
        check_vma=False,
    )
```

```python
import functools

import jax
import jax.numpy as jnp
from jax import lax
from jax.experimental import pallas as pl
from jax.experimental.pallas import tpu as pltpu
from jax.sharding import PartitionSpec as P

decay_unit = 5e-05
rate = decay_unit * 1.4426950408889634
MESH = pl.DeviceIdType.MESH
F32 = jnp.float32
BF = jnp.bfloat16
LANES = 128
SIDE = 4
ORDERS = ((1, 0, 2), (0, 2, 1), (2, 1, 0))
CUTS = (0, 512, 1024, 2048)
WIDE = 2 * LANES
GROUP = 8


def dot(a, b):
    return lax.dot_general(a, b, (((1,), (0,)), ((), ())), preferred_element_type=F32)


def dot_nt(a, b):
    return lax.dot_general(a, b, (((1,), (1,)), ((), ())), preferred_element_type=F32)


def flip(a):
    return a.astype(F32).T


def span(j, size=LANES):
    return pl.ds(pl.multiple_of(j * size, size), size)


def grid_of(rows, columns):
    return (
        lax.broadcasted_iota(jnp.int32, (rows, columns), 0),
        lax.broadcasted_iota(jnp.int32, (rows, columns), 1),
    )


def greet_all(n):
    me, seq = lax.axis_index("ctx"), lax.axis_index("dp")
    barrier = pltpu.get_barrier_semaphore()

    def greet(i, carry):
        pl.semaphore_signal(
            barrier, inc=1, device_id={"ctx": lax.rem(me + 2 * i, n)}, device_id_type=MESH
        )
        return carry

    lax.fori_loop(1, n // 2, greet, 0)
    pl.semaphore_signal(
        barrier, inc=1, device_id={"ctx": me + 1 - 2 * lax.rem(me, 2)}, device_id_type=MESH
    )
    for turn in (1, SIDE - 1):
        pl.semaphore_signal(
            barrier, inc=1, device_id={"dp": lax.rem(seq + turn, SIDE)}, device_id_type=MESH
        )
    return barrier


def copy_to(peer, source, target, sems, first):
    return pltpu.make_async_remote_copy(
        src_ref=source,
        dst_ref=target,
        send_sem=sems.at[first],
        recv_sem=sems.at[first + 1],
        device_id={"ctx": peer},
        device_id_type=MESH,
    )


def finish(n, source, target, sems, first):
    peer = lax.rem(lax.axis_index("ctx") + 2, n)
    some = pl.ds(0, n // 2 - 1)
    copy_to(peer, source.at[some], target.at[some], sems, first).wait()


def in_parts(d):
    high = d.astype(BF).astype(F32)
    middle = (d - high).astype(BF).astype(F32)
    low = d - high - middle
    which, _ = grid_of(16, d.shape[1])
    parts = jnp.where(which == 0, high, jnp.where(which == 1, middle, low))
    return jnp.where(which < 3, parts, 0.0).astype(BF)


def from_parts(rows):
    parts = rows.astype(F32)
    return parts[0:1] + parts[1:2] + parts[2:3]


def accumulate_decay(steps_t, level_t):
    heads, rows = steps_t.shape
    row, column = grid_of(rows, rows)
    ones = jnp.where(row <= column, 1.0, 0.0).astype(BF)
    value = steps_t[...]
    high = (value >> 7).astype(F32).astype(BF)
    low = (value & 127).astype(F32).astype(BF)
    level_t[...] = jnp.zeros_like(level_t)
    level_t[:heads, :] = (dot(high, ones) * 128.0 + dot(low, ones)) * rate


def columns_of(level, q):
    rolled = pltpu.roll(level[...], lax.rem(LANES - 4 * q, LANES), 1)
    return [jnp.broadcast_to(rolled[:, i : i + 1], rolled.shape) for i in range(4)]


def spread(level, q):
    parts = columns_of(level, q)
    _, column = grid_of(*parts[0].shape)
    left = column < LANES // 2
    both = jnp.concatenate(
        [jnp.where(left, parts[0], parts[1]), jnp.where(left, parts[2], parts[3])], axis=1
    )
    return both, both[both.shape[0] - 1 :]


def beside(blocks, q):
    return jnp.concatenate([blocks[2 * q], blocks[2 * q + 1]], axis=1)


def both_of(slabs, q):
    return jnp.concatenate([slabs[0, q], slabs[1, q]], axis=1)


def split_heads(value):
    _, column = grid_of(*value.shape)
    wide = value.astype(F32)
    left = jnp.where(column < LANES // 2, wide, 0.0).astype(BF)
    right = jnp.where(column < LANES // 2, 0.0, wide).astype(BF)
    return jnp.concatenate([left, right], axis=0)


class Gather:
    def __init__(self, shard, whole, own_sem, ring_send, ring_recv, pair_send, pair_recv):
        ctx = lax.axis_index("ctx")
        self.at = (lax.axis_index("dp"), ctx // (2 * SIDE), lax.rem(ctx // 2, SIDE))
        self.core = lax.rem(ctx, 2)
        self.shard, self.whole = shard, whole
        self.own_sem = own_sem
        self.ring_send, self.ring_recv = ring_send, ring_recv
        self.pair_send, self.pair_recv = pair_send, pair_recv

    def device(self, dim, place, core):
        y, x, z = [place if d == dim else v for d, v in enumerate(self.at)]
        return {"dp": y, "ctx": (x * SIDE + z) * 2 + core}

    def region(self, part, phase, place, rows):
        order = ORDERS[part]
        index = list(self.at)
        for dim in order[:phase]:
            index[dim] = slice(None)
        index[order[phase]] = place
        columns = pl.ds(CUTS[part], CUTS[part + 1] - CUTS[part])
        return self.whole.at[(*index, self.core, rows, columns)]

    def ring(self, part, phase, step):
        dim = ORDERS[part][phase]
        here = self.at[dim]
        right, left = lax.rem(here + 1, SIDE), lax.rem(here + SIDE - 1, SIDE)
        rows = self.shard.shape[0]
        for side, (peer, other) in enumerate(((right, left), (left, right))):
            if step == 0:
                piece = self.region(part, phase, here, pl.ds(0, rows))
            else:
                piece = self.region(part, phase, other, pl.ds(side * (rows // 2), rows // 2))
            yield pltpu.make_async_remote_copy(
                src_ref=piece,
                dst_ref=piece,
                send_sem=self.ring_send.at[part, phase, step, side],
                recv_sem=self.ring_recv.at[part, phase, step, side],
                device_id=self.device(dim, peer, self.core),
                device_id_type=MESH,
            )

    def pair(self, part, turn):
        dim = ORDERS[part][2]
        place = lax.rem(self.at[dim] + turn, SIDE)
        piece = self.region(part, 2, place, pl.ds(0, self.shard.shape[0]))
        return pltpu.make_async_remote_copy(
            src_ref=piece,
            dst_ref=piece,
            send_sem=self.pair_send.at[part, turn],
            recv_sem=self.pair_recv.at[part, turn],
            device_id=self.device(None, None, 1 - self.core),
            device_id_type=MESH,
        )

    def post(self, part, number):
        for copy in self.ring(part, number // 2, number % 2):
            copy.start()

    def begin(self):
        own = pltpu.make_async_copy(
            self.shard, self.whole.at[(*self.at, self.core)], self.own_sem.at[0]
        )
        own.start()
        own.wait()
        for part in range(3):
            self.post(part, 0)

    def advance(self, number, parts=(0, 1, 2)):
        turns = {3: (0,), 4: (1, 3), 5: (2,)}.get(number, ())
        for part in parts:
            for copy in self.ring(part, number // 2, number % 2):
                copy.wait()
            if number < 5:
                self.post(part, number + 1)
            for turn in turns:
                self.pair(part, turn).start()

    def end(self, parts, turns=range(SIDE)):
        for part in parts:
            for turn in turns:
                self.pair(part, turn).wait()


def layer_kernel(
    n, scale, x, b, c, steps_t, cot, shard, out, grad_x, grad_b, grad_c,
    level, level_t, masked, masked_t, b_t, c_t, decays, y, send, near, joint, recv, stage, got, give, before, mixed,
    whole, back, dshift, flow, inner_sum, b_sum, c_sum, send2, near2, joint2, recv2, stage2, got2, give2, after,
    falls, tails, shifts,
    sems, own_sem, ring_send, ring_recv, pair_send, pair_recv,
):
    me = lax.axis_index("ctx")
    rows = x.shape[0]
    state = b.shape[1]
    core, chip, chips = lax.rem(me, 2), me // 2, n // 2
    partner = me + 1 - 2 * core
    first = (1 - core).astype(F32)
    second = 1.0 - first
    barrier = greet_all(n)
    gather = Gather(shard, whole, own_sem, ring_send, ring_recv, pair_send, pair_recv)
    pl.semaphore_wait(barrier, n // 2 + 2)
    gather.begin()

    accumulate_decay(steps_t, level_t)
    level[...] = flip(level_t[...])
    row, column = grid_of(rows, rows)
    masked[...] = jnp.where(row >= column, scale * dot_nt(c[...], b[...]), 0.0)
    masked_t[...] = jnp.where(row <= column, scale * dot_nt(b[...], c[...]), 0.0)
    b_t[...] = flip(b[...]).astype(BF)
    c_t[...] = flip(c[...]).astype(BF)
    inner_sum[...] = jnp.zeros_like(inner_sum)
    b_sum[...] = jnp.zeros_like(b_sum)
    c_sum[...] = jnp.zeros_like(c_sum)

    def make_term(q, carry):
        both, last = spread(level, q)
        falls[q] = jnp.exp2(-both)
        tail = jnp.exp2(both - last)
        tails[q] = tail
        shifted = (x[:, span(q, WIDE)].astype(F32) * tail).astype(BF)
        shifts[:, span(q, WIDE)] = shifted
        term = dot(b_t[...], shifted).astype(BF)
        parts = in_parts(jnp.exp2(-last))
        for u in range(2):
            send[u, q, :state] = term[:, u * LANES : (u + 1) * LANES]
            send[u, q, state:] = parts[:, u * LANES : (u + 1) * LANES]
        return carry

    def inside(q, carry):
        columns = columns_of(level, q)
        for u in range(2):
            mix = []
            for v in (2 * u, 2 * u + 1):
                gap = level_t[pl.ds(4 * q + v, 1), :] - columns[v]
                mix.append((masked[...] * jnp.exp2(jnp.minimum(gap, 0.0))).astype(BF))
            y[2 * q + u] = dot(jnp.concatenate(mix, axis=1), split_heads(x[:, span(2 * q + u)]))
        return carry

    gather.advance(0)
    lax.fori_loop(0, n // 8, make_term, 0)
    gather.advance(1)
    lax.fori_loop(n // 8, n // 2, make_term, 0)
    near_terms = copy_to(partner, send.at[1 - core], near, sems, 0)
    near_terms.start()
    gather.advance(2)
    lax.fori_loop(0, n // 8, inside, 0)
    gather.advance(3)
    near_terms.wait()

    def combine(q, carry):
        mine, theirs = from_parts(send[core, q, state:]), from_parts(near[q, state:])
        here = (first * theirs + second) * send[core, q, :state].astype(F32)
        there = (second * mine + first) * near[q, :state].astype(F32)
        joint[q, :state] = (here + there).astype(BF)
        joint[q, state:] = in_parts(mine * theirs)
        return carry

    lax.fori_loop(0, chips, combine, 0)

    def post_term(i, carry):
        q = lax.rem(chip + i, chips)
        copy_to(2 * q + core, joint.at[q], recv.at[chip], sems, 2).start()
        return carry

    lax.fori_loop(1, chips, post_term, 0)
    recv[chip] = joint[chip]
    lax.fori_loop(n // 8, n // 2, inside, 0)
    gather.advance(4)
    finish(n, joint, recv, sems, 2)

    def step(g, carry):
        for u in range(GROUP):
            k = g * GROUP + u
            stage[k] = carry.astype(BF)
            d = from_parts(recv[k, state:])
            decays[k] = jnp.broadcast_to(d, (8, LANES))
            carry = d * carry + recv[k, :state].astype(F32)

        def post(k, nothing):
            @pl.when(k != chip)
            def _():
                copy_to(2 * k + core, stage.at[k], got.at[chip], sems, 4).start()

            return nothing

        lax.fori_loop(g * GROUP, (g + 1) * GROUP, post, 0)
        return carry

    lax.fori_loop(0, chips // GROUP, step, jnp.zeros((state, LANES), F32))
    got[chip] = stage[chip]
    gather.advance(5, (0, 1))
    gather.end((0, 1))

    def place(i):
        row = i // SIDE
        turn = row + (row // 2) * (5 - 2 * row)
        return lax.rem(lax.axis_index("dp") + turn, SIDE) * SIDE + lax.rem(i, SIDE)

    early, late = pl.ds(0, CUTS[2]), pl.ds(CUTS[2], CUTS[3] - CUTS[2])

    def share(q, columns):
        chunk = whole[q // SIDE, lax.rem(q, SIDE), :, :, :, columns]
        return dot_nt(cot[:, columns], chunk.reshape(WIDE, chunk.shape[-1]))

    def begin_back(q, carry):
        part = share(q, early)
        for u in range(2):
            flow[2 * q + u] = part[:, u * LANES : (u + 1) * LANES]
        return carry

    lax.fori_loop(0, n // 2, begin_back, 0)
    finish(n, stage, got, sems, 4)

    def pass_on(q, carry):
        early_state = got[q].astype(F32)
        d = first * from_parts(send[core, q, state:]) + second * from_parts(near[q, state:])
        term = first * send[core, q, :state].astype(F32) + second * near[q, :state].astype(F32)
        late_state = d * early_state + term
        before[core, q] = (first * early_state + second * late_state).astype(BF)
        give[q] = (first * late_state + second * early_state).astype(BF)
        return carry

    lax.fori_loop(0, chips, pass_on, 0)
    near_states = copy_to(partner, give, before.at[core], sems, 6)
    near_states.start()
    gather.end((2,), (0, 1, 3))

    def make_back(i):
        q = place(i)
        back[:, span(q, WIDE)] = (beside(flow, q) + share(q, late)).astype(BF)

    def make_term_back(i):
        q = place(i)
        shift = (back[:, span(q, WIDE)].astype(F32) * falls[q]).astype(BF)
        dshift[:, span(q, WIDE)] = shift
        term = dot(c_t[...], shift).astype(BF)
        for u in range(2):
            send2[u, q] = term[:, u * LANES : (u + 1) * LANES]

    def post_back(i):
        q = place(i)
        copy_to(partner, send2.at[1 - core, q], near2.at[q], sems, 8).start()

    def send_term(i, carry):
        make_term_back(i - 1)
        make_back(i)
        post_back(i - 1)
        return carry

    make_back(0)
    lax.fori_loop(1, 2 * SIDE, send_term, 0)
    gather.advance(5, (2,))
    lax.fori_loop(2 * SIDE, 3 * SIDE, send_term, 0)
    gather.end((2,), (2,))
    lax.fori_loop(3 * SIDE, n // 2, send_term, 0)
    make_term_back(n // 2 - 1)
    post_back(n // 2 - 1)
    copy_to(partner, send2.at[1 - core], near2, sems, 8).wait()

    def combine_back(i, carry):
        q = lax.rem(chip + 1 + i, chips)
        mine, theirs = from_parts(send[core, q, state:]), from_parts(near[q, state:])
        here = (first + second * theirs) * send2[core, q].astype(F32)
        there = (first * mine + second) * near2[q].astype(F32)
        joint2[q] = (here + there).astype(BF)

        @pl.when(q != chip)
        def _():
            copy_to(2 * q + core, joint2.at[q], recv2.at[chip], sems, 10).start()

        return carry

    lax.fori_loop(0, chips, combine_back, 0)
    recv2[chip] = joint2[chip]
    near_states.wait()

    def inside_back(q, carry):
        columns = columns_of(level, q)
        total = inner_sum[...]
        for u in range(2):
            j = 2 * q + u
            part = back[:, span(j)]
            pair = dot_nt(split_heads(x[:, span(j)]), part)
            mix = []
            for v in range(2):
                gap = columns[2 * u + v] - level_t[pl.ds(4 * q + 2 * u + v, 1), :]
                fade = jnp.exp2(jnp.minimum(gap, 0.0))
                mix.append((masked_t[...] * fade).astype(BF))
                total = total + fade * pair[v * rows : (v + 1) * rows]
            flow[j] = dot(jnp.concatenate(mix, axis=1), split_heads(part))
        inner_sum[...] = total
        c_sum[...] += dot_nt(dshift[:, span(q, WIDE)], both_of(before, q))
        return carry

    lax.fori_loop(0, n // 2, inside_back, 0)
    finish(n, joint2, recv2, sems, 10)

    def step_back(g, carry):
        for u in range(GROUP):
            k = chips - 1 - (g * GROUP + u)
            stage2[k] = carry.astype(BF)
            carry = decays[k, 0:1] * carry + recv2[k].astype(F32)

        def post(i, nothing):
            k = chips - 1 - i

            @pl.when(k != chip)
            def _():
                copy_to(2 * k + core, stage2.at[k], got2.at[chip], sems, 12).start()

            return nothing

        lax.fori_loop(g * GROUP, (g + 1) * GROUP, post, 0)
        return carry

    lax.fori_loop(0, chips // GROUP, step_back, jnp.zeros((state, LANES), F32))
    got2[chip] = stage2[chip]

    def join(q, carry):
        carried = scale * falls[q] * dot(c[...], both_of(before, q))
        mixed[:, span(q, WIDE)] = (beside(y, q) + carried).astype(BF)
        return carry

    lax.fori_loop(0, n // 2, join, 0)

    finish(n, stage2, got2, sems, 12)

    def pass_back(q, carry):
        late_state = got2[q].astype(F32)
        d = first * from_parts(near[q, state:]) + second * from_parts(send[core, q, state:])
        term = first * near2[q].astype(F32) + second * send2[core, q].astype(F32)
        early_state = d * late_state + term
        after[core, q] = (first * early_state + second * late_state).astype(BF)
        give2[q] = (first * late_state + second * early_state).astype(BF)
        return carry

    lax.fori_loop(0, chips, pass_back, 0)
    near_after = copy_to(partner, give2, after.at[core], sems, 14)
    near_after.start()

    def project(i, carry):
        chunk = whole[:, :, :, :, :, span(i, 256)].reshape(x.shape[1], 256)
        out[:, span(i, 256)] = dot(mixed[...], chunk).astype(BF)
        return carry

    lax.fori_loop(0, out.shape[1] // 256, project, 0)
    kernel_t = jnp.where(row <= column, scale * inner_sum[...], 0.0)
    kernel = kernel_t.T.astype(BF)
    grad_c[...] = (dot(kernel, b[...]) + scale * c_sum[...]).astype(BF)
    near_after.wait()

    def join_back(q, carry):
        late = both_of(after, q)
        carried = scale * tails[q] * dot(b[...], late)
        grad_x[:, span(q, WIDE)] = (beside(flow, q) + carried).astype(BF)
        b_sum[...] += dot_nt(shifts[:, span(q, WIDE)], late)
        return carry

    lax.fori_loop(0, n // 2, join_back, 0)
    grad_b[...] = (dot(kernel_t.astype(BF), c[...]) + scale * b_sum[...]).astype(BF)


def body(x_in, b_in, c_in, log_decay, w_out, cotangent):
    x, b, c, steps, cot = x_in[0], b_in[0], c_in[0], log_decay[0], cotangent[0]
    rows = x.shape[0]
    state = b.shape[1]
    n = lax.axis_size("ctx")
    scale = (state * rows * n) ** (-0.5)
    vmem = pl.BlockSpec(memory_space=pltpu.VMEM)
    shape = jax.ShapeDtypeStruct
    square = pltpu.VMEM((rows, rows), F32)
    turned = pltpu.VMEM((state, rows), BF)
    blocks = pltpu.VMEM((n // 2, state, LANES), BF)
    marked = pltpu.VMEM((n // 2, state + 16, LANES), BF)
    slabs = pltpu.VMEM((2, n // 2, state, LANES), BF)
    marked_slabs = pltpu.VMEM((2, n // 2, state + 16, LANES), BF)
    parts = pltpu.VMEM((n, rows, LANES), F32)
    wide = pltpu.VMEM(x.shape, BF)
    spreads = pltpu.VMEM((n // 2, rows, WIDE), F32)
    sums = pltpu.VMEM((rows, state), F32)
    ring = pltpu.SemaphoreType.DMA((3, 3, 2, 2))
    pair = pltpu.SemaphoreType.DMA((3, SIDE))
    results = pl.pallas_call(
        functools.partial(layer_kernel, n, scale),
        out_shape=(
            shape(cot.shape, BF), shape(x.shape, BF), shape(b.shape, BF), shape(c.shape, BF),
        ),
        in_specs=[vmem] * 6,
        out_specs=(vmem,) * 4,
        scratch_shapes=[
            square, square, square, square, turned, turned,
            pltpu.VMEM((n // 2, 8, LANES), F32),
            parts, marked_slabs, marked, marked, marked, blocks, blocks, blocks, slabs, wide,
            pltpu.VMEM((SIDE, SIDE, SIDE, 2) + w_out.shape, BF),
            wide, wide, parts, square, sums, sums,
            slabs, blocks, blocks, blocks, blocks, blocks, blocks, slabs,
            spreads, spreads, wide,
            pltpu.SemaphoreType.DMA((16,)),
            pltpu.SemaphoreType.DMA((1,)),
            ring, ring, pair, pair,
        ],
        compiler_params=pltpu.CompilerParams(
            collective_id=0, has_side_effects=True, vmem_limit_bytes=60 * 1024 * 1024
        ),
        name="layer",
    )(x, b, c, steps.T, cot, w_out)
    return tuple(r[None] for r in results)


def solution(mesh):
    tokens = P("dp", "ctx", None)
    return jax.shard_map(
        body,
        mesh=mesh,
        in_specs=(tokens, tokens, tokens, tokens, P(("dp", "ctx"), None), tokens),
        out_specs=(tokens, tokens, tokens, tokens),
        check_vma=False,
    )
```

```python
import functools

import jax
import jax.numpy as jnp
from jax import lax
from jax.experimental import pallas as pl
from jax.experimental.pallas import tpu as pltpu
from jax.sharding import PartitionSpec as P

decay_unit = 5e-05
rate = decay_unit * 1.4426950408889634
MESH = pl.DeviceIdType.MESH
F32 = jnp.float32
BF = jnp.bfloat16
LANES = 128
SIDE = 4
ORDERS = ((1, 0, 2), (0, 2, 1), (2, 1, 0))
CUTS = (0, 512, 1024, 2048)
WIDE = 2 * LANES
GROUP = 8


def dot(a, b):
    return lax.dot_general(a, b, (((1,), (0,)), ((), ())), preferred_element_type=F32)


def dot_nt(a, b):
    return lax.dot_general(a, b, (((1,), (1,)), ((), ())), preferred_element_type=F32)


def flip(a):
    return a.astype(F32).T


def span(j, size=LANES):
    return pl.ds(pl.multiple_of(j * size, size), size)


def grid_of(rows, columns):
    return (
        lax.broadcasted_iota(jnp.int32, (rows, columns), 0),
        lax.broadcasted_iota(jnp.int32, (rows, columns), 1),
    )


def greet_all(n):
    me, seq = lax.axis_index("ctx"), lax.axis_index("dp")
    barrier = pltpu.get_barrier_semaphore()

    def greet(i, carry):
        pl.semaphore_signal(
            barrier, inc=1, device_id={"ctx": lax.rem(me + 2 * i, n)}, device_id_type=MESH
        )
        return carry

    lax.fori_loop(1, n // 2, greet, 0)
    pl.semaphore_signal(
        barrier, inc=1, device_id={"ctx": me + 1 - 2 * lax.rem(me, 2)}, device_id_type=MESH
    )
    for turn in (1, SIDE - 1):
        pl.semaphore_signal(
            barrier, inc=1, device_id={"dp": lax.rem(seq + turn, SIDE)}, device_id_type=MESH
        )
    return barrier


def copy_to(peer, source, target, sems, first):
    return pltpu.make_async_remote_copy(
        src_ref=source,
        dst_ref=target,
        send_sem=sems.at[first],
        recv_sem=sems.at[first + 1],
        device_id={"ctx": peer},
        device_id_type=MESH,
    )


def finish(n, source, target, sems, first):
    peer = lax.rem(lax.axis_index("ctx") + 2, n)
    some = pl.ds(0, n // 2 - 1)
    copy_to(peer, source.at[some], target.at[some], sems, first).wait()


def in_parts(d):
    high = d.astype(BF).astype(F32)
    middle = (d - high).astype(BF).astype(F32)
    low = d - high - middle
    which, _ = grid_of(16, d.shape[1])
    parts = jnp.where(which == 0, high, jnp.where(which == 1, middle, low))
    return jnp.where(which < 3, parts, 0.0).astype(BF)


def from_parts(rows):
    parts = rows.astype(F32)
    return parts[0:1] + parts[1:2] + parts[2:3]


def accumulate_decay(steps_t, level_t):
    heads, rows = steps_t.shape
    row, column = grid_of(rows, rows)
    ones = jnp.where(row <= column, 1.0, 0.0).astype(BF)
    value = steps_t[...]
    high = (value >> 7).astype(F32).astype(BF)
    low = (value & 127).astype(F32).astype(BF)
    level_t[...] = jnp.zeros_like(level_t)
    level_t[:heads, :] = (dot(high, ones) * 128.0 + dot(low, ones)) * rate


def columns_of(level, q):
    rolled = pltpu.roll(level[...], lax.rem(LANES - 4 * q, LANES), 1)
    return [jnp.broadcast_to(rolled[:, i : i + 1], rolled.shape) for i in range(4)]


def spread(level, q):
    parts = columns_of(level, q)
    _, column = grid_of(*parts[0].shape)
    left = column < LANES // 2
    both = jnp.concatenate(
        [jnp.where(left, parts[0], parts[1]), jnp.where(left, parts[2], parts[3])], axis=1
    )
    return both, both[both.shape[0] - 1 :]


def beside(blocks, q):
    return jnp.concatenate([blocks[2 * q], blocks[2 * q + 1]], axis=1)


def both_of(slabs, q):
    return jnp.concatenate([slabs[0, q], slabs[1, q]], axis=1)


def split_heads(value):
    _, column = grid_of(*value.shape)
    wide = value.astype(F32)
    left = jnp.where(column < LANES // 2, wide, 0.0).astype(BF)
    right = jnp.where(column < LANES // 2, 0.0, wide).astype(BF)
    return jnp.concatenate([left, right], axis=0)


class Gather:
    def __init__(self, shard, whole, own_sem, ring_send, ring_recv, pair_send, pair_recv):
        ctx = lax.axis_index("ctx")
        self.at = (lax.axis_index("dp"), ctx // (2 * SIDE), lax.rem(ctx // 2, SIDE))
        self.core = lax.rem(ctx, 2)
        self.shard, self.whole = shard, whole
        self.own_sem = own_sem
        self.ring_send, self.ring_recv = ring_send, ring_recv
        self.pair_send, self.pair_recv = pair_send, pair_recv

    def device(self, dim, place, core):
        y, x, z = [place if d == dim else v for d, v in enumerate(self.at)]
        return {"dp": y, "ctx": (x * SIDE + z) * 2 + core}

    def region(self, part, phase, place, rows):
        order = ORDERS[part]
        index = list(self.at)
        for dim in order[:phase]:
            index[dim] = slice(None)
        index[order[phase]] = place
        columns = pl.ds(CUTS[part], CUTS[part + 1] - CUTS[part])
        return self.whole.at[(*index, self.core, rows, columns)]

    def ring(self, part, phase, step):
        dim = ORDERS[part][phase]
        here = self.at[dim]
        right, left = lax.rem(here + 1, SIDE), lax.rem(here + SIDE - 1, SIDE)
        rows = self.shard.shape[0]
        for side, (peer, other) in enumerate(((right, left), (left, right))):
            if step == 0:
                piece = self.region(part, phase, here, pl.ds(0, rows))
            else:
                piece = self.region(part, phase, other, pl.ds(side * (rows // 2), rows // 2))
            yield pltpu.make_async_remote_copy(
                src_ref=piece,
                dst_ref=piece,
                send_sem=self.ring_send.at[part, phase, step, side],
                recv_sem=self.ring_recv.at[part, phase, step, side],
                device_id=self.device(dim, peer, self.core),
                device_id_type=MESH,
            )

    def pair(self, part, turn):
        dim = ORDERS[part][2]
        place = lax.rem(self.at[dim] + turn, SIDE)
        piece = self.region(part, 2, place, pl.ds(0, self.shard.shape[0]))
        return pltpu.make_async_remote_copy(
            src_ref=piece,
            dst_ref=piece,
            send_sem=self.pair_send.at[part, turn],
            recv_sem=self.pair_recv.at[part, turn],
            device_id=self.device(None, None, 1 - self.core),
            device_id_type=MESH,
        )

    def post(self, part, number):
        for copy in self.ring(part, number // 2, number % 2):
            copy.start()

    def begin(self):
        own = pltpu.make_async_copy(
            self.shard, self.whole.at[(*self.at, self.core)], self.own_sem.at[0]
        )
        own.start()
        own.wait()
        for part in range(3):
            self.post(part, 0)

    def advance(self, number, parts=(0, 1, 2)):
        turns = {3: (0,), 4: (1, 3), 5: (2,)}.get(number, ())
        for part in parts:
            for copy in self.ring(part, number // 2, number % 2):
                copy.wait()
            if number < 5:
                self.post(part, number + 1)
            for turn in turns:
                self.pair(part, turn).start()

    def end(self, parts, turns=range(SIDE)):
        for part in parts:
            for turn in turns:
                self.pair(part, turn).wait()


def layer_kernel(
    n, scale, x, b, c, steps_t, cot, shard, out, grad_x, grad_b, grad_c,
    level, level_t, masked, masked_t, b_t, c_t, decays, y, send, near, joint, recv, stage, got, give, before, mixed,
    whole, back, dshift, flow, inner_sum, b_sum, c_sum, send2, near2, joint2, recv2, stage2, got2, give2, after,
    falls, tails, shifts,
    sems, own_sem, ring_send, ring_recv, pair_send, pair_recv,
):
    me = lax.axis_index("ctx")
    rows = x.shape[0]
    state = b.shape[1]
    core, chip, chips = lax.rem(me, 2), me // 2, n // 2
    partner = me + 1 - 2 * core
    first = (1 - core).astype(F32)
    second = 1.0 - first
    barrier = greet_all(n)
    gather = Gather(shard, whole, own_sem, ring_send, ring_recv, pair_send, pair_recv)
    pl.semaphore_wait(barrier, n // 2 + 2)
    gather.begin()

    accumulate_decay(steps_t, level_t)
    level[...] = flip(level_t[...])
    row, column = grid_of(rows, rows)
    masked[...] = jnp.where(row >= column, scale * dot_nt(c[...], b[...]), 0.0)
    masked_t[...] = jnp.where(row <= column, scale * dot_nt(b[...], c[...]), 0.0)
    b_t[...] = flip(b[...]).astype(BF)
    c_t[...] = flip(c[...]).astype(BF)
    inner_sum[...] = jnp.zeros_like(inner_sum)
    b_sum[...] = jnp.zeros_like(b_sum)
    c_sum[...] = jnp.zeros_like(c_sum)

    def make_term(q, carry):
        both, last = spread(level, q)
        falls[q] = jnp.exp2(-both)
        tail = jnp.exp2(both - last)
        tails[q] = tail
        shifted = (x[:, span(q, WIDE)].astype(F32) * tail).astype(BF)
        shifts[:, span(q, WIDE)] = shifted
        term = dot(b_t[...], shifted).astype(BF)
        parts = in_parts(jnp.exp2(-last))
        for u in range(2):
            send[u, q, :state] = term[:, u * LANES : (u + 1) * LANES]
            send[u, q, state:] = parts[:, u * LANES : (u + 1) * LANES]
        return carry

    def inside(q, carry):
        columns = columns_of(level, q)
        for u in range(2):
            mix = []
            for v in (2 * u, 2 * u + 1):
                gap = level_t[pl.ds(4 * q + v, 1), :] - columns[v]
                mix.append((masked[...] * jnp.exp2(jnp.minimum(gap, 0.0))).astype(BF))
            y[2 * q + u] = dot(jnp.concatenate(mix, axis=1), split_heads(x[:, span(2 * q + u)]))
        return carry

    gather.advance(0)
    lax.fori_loop(0, n // 8, make_term, 0)
    gather.advance(1)
    lax.fori_loop(n // 8, n // 2, make_term, 0)
    near_terms = copy_to(partner, send.at[1 - core], near, sems, 0)
    near_terms.start()
    gather.advance(2)
    lax.fori_loop(0, n // 8, inside, 0)
    gather.advance(3)
    near_terms.wait()

    def combine(q, carry):
        mine, theirs = from_parts(send[core, q, state:]), from_parts(near[q, state:])
        here = (first * theirs + second) * send[core, q, :state].astype(F32)
        there = (second * mine + first) * near[q, :state].astype(F32)
        joint[q, :state] = (here + there).astype(BF)
        joint[q, state:] = in_parts(mine * theirs)
        return carry

    lax.fori_loop(0, chips, combine, 0)

    def post_term(i, carry):
        q = lax.rem(chip + i, chips)
        copy_to(2 * q + core, joint.at[q], recv.at[chip], sems, 2).start()
        return carry

    lax.fori_loop(1, chips, post_term, 0)
    recv[chip] = joint[chip]
    lax.fori_loop(n // 8, n // 2, inside, 0)
    gather.advance(4)
    finish(n, joint, recv, sems, 2)

    def step(g, carry):
        for u in range(GROUP):
            k = g * GROUP + u
            stage[k] = carry.astype(BF)
            d = from_parts(recv[k, state:])
            decays[k] = jnp.broadcast_to(d, (8, LANES))
            carry = d * carry + recv[k, :state].astype(F32)

        def post(k, nothing):
            @pl.when(k != chip)
            def _():
                copy_to(2 * k + core, stage.at[k], got.at[chip], sems, 4).start()

            return nothing

        lax.fori_loop(g * GROUP, (g + 1) * GROUP, post, 0)
        return carry

    lax.fori_loop(0, chips // GROUP, step, jnp.zeros((state, LANES), F32))
    got[chip] = stage[chip]
    gather.advance(5, (0, 1))
    gather.end((0, 1))

    def place(i):
        row = i // SIDE
        turn = row + (row // 2) * (5 - 2 * row)
        return lax.rem(lax.axis_index("dp") + turn, SIDE) * SIDE + lax.rem(i, SIDE)

    early, late = pl.ds(0, CUTS[2]), pl.ds(CUTS[2], CUTS[3] - CUTS[2])

    def share(q, columns):
        chunk = whole[q // SIDE, lax.rem(q, SIDE), :, :, :, columns]
        return dot_nt(cot[:, columns], chunk.reshape(WIDE, chunk.shape[-1]))

    def begin_back(q, carry):
        part = share(q, early)
        for u in range(2):
            flow[2 * q + u] = part[:, u * LANES : (u + 1) * LANES]
        return carry

    lax.fori_loop(0, n // 2, begin_back, 0)
    finish(n, stage, got, sems, 4)

    def pass_on(q, carry):
        early_state = got[q].astype(F32)
        d = first * from_parts(send[core, q, state:]) + second * from_parts(near[q, state:])
        term = first * send[core, q, :state].astype(F32) + second * near[q, :state].astype(F32)
        late_state = d * early_state + term
        before[core, q] = (first * early_state + second * late_state).astype(BF)
        give[q] = (first * late_state + second * early_state).astype(BF)
        return carry

    lax.fori_loop(0, chips, pass_on, 0)
    near_states = copy_to(partner, give, before.at[core], sems, 6)
    near_states.start()
    gather.end((2,), (0, 1, 3))

    def make_back(i):
        q = place(i)
        back[:, span(q, WIDE)] = (beside(flow, q) + share(q, late)).astype(BF)

    def make_term_back(i):
        q = place(i)
        shift = (back[:, span(q, WIDE)].astype(F32) * falls[q]).astype(BF)
        dshift[:, span(q, WIDE)] = shift
        term = dot(c_t[...], shift).astype(BF)
        for u in range(2):
            send2[u, q] = term[:, u * LANES : (u + 1) * LANES]

    def post_back(i):
        q = place(i)
        copy_to(partner, send2.at[1 - core, q], near2.at[q], sems, 8).start()

    def send_term(i, carry):
        make_term_back(i - 1)
        make_back(i)
        post_back(i - 1)
        return carry

    make_back(0)
    lax.fori_loop(1, 2 * SIDE, send_term, 0)
    gather.advance(5, (2,))
    lax.fori_loop(2 * SIDE, 3 * SIDE, send_term, 0)
    gather.end((2,), (2,))
    lax.fori_loop(3 * SIDE, n // 2, send_term, 0)
    make_term_back(n // 2 - 1)
    post_back(n // 2 - 1)
    copy_to(partner, send2.at[1 - core], near2, sems, 8).wait()

    def combine_back(i, carry):
        q = lax.rem(chip + 1 + i, chips)
        mine, theirs = from_parts(send[core, q, state:]), from_parts(near[q, state:])
        here = (first + second * theirs) * send2[core, q].astype(F32)
        there = (first * mine + second) * near2[q].astype(F32)
        joint2[q] = (here + there).astype(BF)

        @pl.when(q != chip)
        def _():
            copy_to(2 * q + core, joint2.at[q], recv2.at[chip], sems, 10).start()

        return carry

    lax.fori_loop(0, chips, combine_back, 0)
    recv2[chip] = joint2[chip]
    near_states.wait()

    def inside_back(q, carry):
        columns = columns_of(level, q)
        total = inner_sum[...]
        for u in range(2):
            j = 2 * q + u
            part = back[:, span(j)]
            pair = dot_nt(split_heads(x[:, span(j)]), part)
            mix = []
            for v in range(2):
                gap = columns[2 * u + v] - level_t[pl.ds(4 * q + 2 * u + v, 1), :]
                fade = jnp.exp2(jnp.minimum(gap, 0.0))
                mix.append((masked_t[...] * fade).astype(BF))
                total = total + fade * pair[v * rows : (v + 1) * rows]
            flow[j] = dot(jnp.concatenate(mix, axis=1), split_heads(part))
        inner_sum[...] = total
        c_sum[...] += dot_nt(dshift[:, span(q, WIDE)], both_of(before, q))
        return carry

    held = n // 2 - 5
    lax.fori_loop(0, held, inside_back, 0)
    finish(n, joint2, recv2, sems, 10)

    def step_back(g, carry):
        for u in range(GROUP):
            k = chips - 1 - (g * GROUP + u)
            stage2[k] = carry.astype(BF)
            carry = decays[k, 0:1] * carry + recv2[k].astype(F32)

        def post(i, nothing):
            k = chips - 1 - i

            @pl.when(k != chip)
            def _():
                copy_to(2 * k + core, stage2.at[k], got2.at[chip], sems, 12).start()

            return nothing

        lax.fori_loop(g * GROUP, (g + 1) * GROUP, post, 0)
        return carry

    lax.fori_loop(0, chips // GROUP, step_back, jnp.zeros((state, LANES), F32))
    got2[chip] = stage2[chip]
    lax.fori_loop(held, n // 2, inside_back, 0)

    def join(q, carry):
        carried = scale * falls[q] * dot(c[...], both_of(before, q))
        mixed[:, span(q, WIDE)] = (beside(y, q) + carried).astype(BF)
        return carry

    lax.fori_loop(0, n // 2, join, 0)

    def project(i, carry):
        chunk = whole[:, :, :, :, :, span(i, WIDE)].reshape(x.shape[1], WIDE)
        out[:, span(i, WIDE)] = dot(mixed[...], chunk).astype(BF)
        return carry

    tiles = out.shape[1] // WIDE
    lax.fori_loop(0, 2, project, 0)
    finish(n, stage2, got2, sems, 12)

    def pass_back(q, carry):
        late_state = got2[q].astype(F32)
        d = first * from_parts(near[q, state:]) + second * from_parts(send[core, q, state:])
        term = first * near2[q].astype(F32) + second * send2[core, q].astype(F32)
        early_state = d * late_state + term
        after[core, q] = (first * early_state + second * late_state).astype(BF)
        give2[q] = (first * late_state + second * early_state).astype(BF)
        return carry

    lax.fori_loop(0, chips, pass_back, 0)
    near_after = copy_to(partner, give2, after.at[core], sems, 14)
    near_after.start()

    lax.fori_loop(2, tiles, project, 0)
    kernel_t = jnp.where(row <= column, scale * inner_sum[...], 0.0)
    kernel = kernel_t.T.astype(BF)
    grad_c[...] = (dot(kernel, b[...]) + scale * c_sum[...]).astype(BF)
    near_after.wait()

    def join_back(q, carry):
        late = both_of(after, q)
        carried = scale * tails[q] * dot(b[...], late)
        grad_x[:, span(q, WIDE)] = (beside(flow, q) + carried).astype(BF)
        b_sum[...] += dot_nt(shifts[:, span(q, WIDE)], late)
        return carry

    lax.fori_loop(0, n // 2, join_back, 0)
    grad_b[...] = (dot(kernel_t.astype(BF), c[...]) + scale * b_sum[...]).astype(BF)


def body(x_in, b_in, c_in, log_decay, w_out, cotangent):
    x, b, c, steps, cot = x_in[0], b_in[0], c_in[0], log_decay[0], cotangent[0]
    rows = x.shape[0]
    state = b.shape[1]
    n = lax.axis_size("ctx")
    scale = (state * rows * n) ** (-0.5)
    vmem = pl.BlockSpec(memory_space=pltpu.VMEM)
    shape = jax.ShapeDtypeStruct
    square = pltpu.VMEM((rows, rows), F32)
    turned = pltpu.VMEM((state, rows), BF)
    blocks = pltpu.VMEM((n // 2, state, LANES), BF)
    marked = pltpu.VMEM((n // 2, state + 16, LANES), BF)
    slabs = pltpu.VMEM((2, n // 2, state, LANES), BF)
    marked_slabs = pltpu.VMEM((2, n // 2, state + 16, LANES), BF)
    parts = pltpu.VMEM((n, rows, LANES), F32)
    wide = pltpu.VMEM(x.shape, BF)
    spreads = pltpu.VMEM((n // 2, rows, WIDE), F32)
    sums = pltpu.VMEM((rows, state), F32)
    ring = pltpu.SemaphoreType.DMA((3, 3, 2, 2))
    pair = pltpu.SemaphoreType.DMA((3, SIDE))
    results = pl.pallas_call(
        functools.partial(layer_kernel, n, scale),
        out_shape=(
            shape(cot.shape, BF), shape(x.shape, BF), shape(b.shape, BF), shape(c.shape, BF),
        ),
        in_specs=[vmem] * 6,
        out_specs=(vmem,) * 4,
        scratch_shapes=[
            square, square, square, square, turned, turned,
            pltpu.VMEM((n // 2, 8, LANES), F32),
            parts, marked_slabs, marked, marked, marked, blocks, blocks, blocks, slabs, wide,
            pltpu.VMEM((SIDE, SIDE, SIDE, 2) + w_out.shape, BF),
            wide, wide, parts, square, sums, sums,
            slabs, blocks, blocks, blocks, blocks, blocks, blocks, slabs,
            spreads, spreads, wide,
            pltpu.SemaphoreType.DMA((16,)),
            pltpu.SemaphoreType.DMA((1,)),
            ring, ring, pair, pair,
        ],
        compiler_params=pltpu.CompilerParams(
            collective_id=0, has_side_effects=True, vmem_limit_bytes=60 * 1024 * 1024
        ),
        name="layer",
    )(x, b, c, steps.T, cot, w_out)
    return tuple(r[None] for r in results)


def solution(mesh):
    tokens = P("dp", "ctx", None)
    return jax.shard_map(
        body,
        mesh=mesh,
        in_specs=(tokens, tokens, tokens, tokens, P(("dp", "ctx"), None), tokens),
        out_specs=(tokens, tokens, tokens, tokens),
        check_vma=False,
    )
```

```python
import functools

import jax
import jax.numpy as jnp
from jax import lax
from jax.experimental import pallas as pl
from jax.experimental.pallas import tpu as pltpu
from jax.sharding import PartitionSpec as P

decay_unit = 5e-05
rate = decay_unit * 1.4426950408889634
MESH = pl.DeviceIdType.MESH
F32 = jnp.float32
BF = jnp.bfloat16
LANES = 128
SIDE = 4
ORDERS = ((1, 0, 2), (0, 2, 1), (2, 1, 0))
CUTS = (0, 512, 1024, 2048)
WIDE = 2 * LANES
GROUP = 8


def dot(a, b):
    return lax.dot_general(a, b, (((1,), (0,)), ((), ())), preferred_element_type=F32)


def dot_nt(a, b):
    return lax.dot_general(a, b, (((1,), (1,)), ((), ())), preferred_element_type=F32)


def flip(a):
    return a.astype(F32).T


def span(j, size=LANES):
    return pl.ds(pl.multiple_of(j * size, size), size)


def grid_of(rows, columns):
    return (
        lax.broadcasted_iota(jnp.int32, (rows, columns), 0),
        lax.broadcasted_iota(jnp.int32, (rows, columns), 1),
    )


def greet_all(n):
    me, seq = lax.axis_index("ctx"), lax.axis_index("dp")
    barrier = pltpu.get_barrier_semaphore()

    def greet(i, carry):
        pl.semaphore_signal(
            barrier, inc=1, device_id={"ctx": lax.rem(me + 2 * i, n)}, device_id_type=MESH
        )
        return carry

    lax.fori_loop(1, n // 2, greet, 0)
    pl.semaphore_signal(
        barrier, inc=1, device_id={"ctx": me + 1 - 2 * lax.rem(me, 2)}, device_id_type=MESH
    )
    for turn in (1, SIDE - 1):
        pl.semaphore_signal(
            barrier, inc=1, device_id={"dp": lax.rem(seq + turn, SIDE)}, device_id_type=MESH
        )
    return barrier


def copy_to(peer, source, target, sems, first):
    return pltpu.make_async_remote_copy(
        src_ref=source,
        dst_ref=target,
        send_sem=sems.at[first],
        recv_sem=sems.at[first + 1],
        device_id={"ctx": peer},
        device_id_type=MESH,
    )


def finish(n, source, target, sems, first):
    peer = lax.rem(lax.axis_index("ctx") + 2, n)
    some = pl.ds(0, n // 2 - 1)
    copy_to(peer, source.at[some], target.at[some], sems, first).wait()


def in_parts(d):
    high = d.astype(BF).astype(F32)
    middle = (d - high).astype(BF).astype(F32)
    low = d - high - middle
    which, _ = grid_of(16, d.shape[1])
    parts = jnp.where(which == 0, high, jnp.where(which == 1, middle, low))
    return jnp.where(which < 3, parts, 0.0).astype(BF)


def from_parts(rows):
    parts = rows.astype(F32)
    return parts[0:1] + parts[1:2] + parts[2:3]


def accumulate_decay(steps_t, level_t):
    heads, rows = steps_t.shape
    row, column = grid_of(rows, rows)
    ones = jnp.where(row <= column, 1.0, 0.0).astype(BF)
    value = steps_t[...]
    high = (value >> 7).astype(F32).astype(BF)
    low = (value & 127).astype(F32).astype(BF)
    level_t[...] = jnp.zeros_like(level_t)
    level_t[:heads, :] = (dot(high, ones) * 128.0 + dot(low, ones)) * rate


def columns_of(level, q):
    rolled = pltpu.roll(level[...], lax.rem(LANES - 4 * q, LANES), 1)
    return [jnp.broadcast_to(rolled[:, i : i + 1], rolled.shape) for i in range(4)]


def spread(level, q):
    parts = columns_of(level, q)
    _, column = grid_of(*parts[0].shape)
    left = column < LANES // 2
    both = jnp.concatenate(
        [jnp.where(left, parts[0], parts[1]), jnp.where(left, parts[2], parts[3])], axis=1
    )
    return both, both[both.shape[0] - 1 :]


def beside(blocks, q):
    return jnp.concatenate([blocks[2 * q], blocks[2 * q + 1]], axis=1)


def both_of(slabs, q):
    return jnp.concatenate([slabs[0, q], slabs[1, q]], axis=1)


def split_heads(value):
    _, column = grid_of(*value.shape)
    wide = value.astype(F32)
    left = jnp.where(column < LANES // 2, wide, 0.0).astype(BF)
    right = jnp.where(column < LANES // 2, 0.0, wide).astype(BF)
    return jnp.concatenate([left, right], axis=0)


class Gather:
    def __init__(self, shard, whole, own_sem, ring_send, ring_recv, pair_send, pair_recv):
        ctx = lax.axis_index("ctx")
        self.at = (lax.axis_index("dp"), ctx // (2 * SIDE), lax.rem(ctx // 2, SIDE))
        self.core = lax.rem(ctx, 2)
        self.shard, self.whole = shard, whole
        self.own_sem = own_sem
        self.ring_send, self.ring_recv = ring_send, ring_recv
        self.pair_send, self.pair_recv = pair_send, pair_recv

    def device(self, dim, place, core):
        y, x, z = [place if d == dim else v for d, v in enumerate(self.at)]
        return {"dp": y, "ctx": (x * SIDE + z) * 2 + core}

    def region(self, part, phase, place, rows):
        order = ORDERS[part]
        index = list(self.at)
        for dim in order[:phase]:
            index[dim] = slice(None)
        index[order[phase]] = place
        columns = pl.ds(CUTS[part], CUTS[part + 1] - CUTS[part])
        return self.whole.at[(*index, self.core, rows, columns)]

    def ring(self, part, phase, step):
        dim = ORDERS[part][phase]
        here = self.at[dim]
        right, left = lax.rem(here + 1, SIDE), lax.rem(here + SIDE - 1, SIDE)
        rows = self.shard.shape[0]
        for side, (peer, other) in enumerate(((right, left), (left, right))):
            if step == 0:
                piece = self.region(part, phase, here, pl.ds(0, rows))
            else:
                piece = self.region(part, phase, other, pl.ds(side * (rows // 2), rows // 2))
            yield pltpu.make_async_remote_copy(
                src_ref=piece,
                dst_ref=piece,
                send_sem=self.ring_send.at[part, phase, step, side],
                recv_sem=self.ring_recv.at[part, phase, step, side],
                device_id=self.device(dim, peer, self.core),
                device_id_type=MESH,
            )

    def pair(self, part, turn):
        dim = ORDERS[part][2]
        place = lax.rem(self.at[dim] + turn, SIDE)
        piece = self.region(part, 2, place, pl.ds(0, self.shard.shape[0]))
        return pltpu.make_async_remote_copy(
            src_ref=piece,
            dst_ref=piece,
            send_sem=self.pair_send.at[part, turn],
            recv_sem=self.pair_recv.at[part, turn],
            device_id=self.device(None, None, 1 - self.core),
            device_id_type=MESH,
        )

    def post(self, part, number):
        for copy in self.ring(part, number // 2, number % 2):
            copy.start()

    def begin(self):
        own = pltpu.make_async_copy(
            self.shard, self.whole.at[(*self.at, self.core)], self.own_sem.at[0]
        )
        own.start()
        own.wait()
        for part in range(3):
            self.post(part, 0)

    def advance(self, number, parts=(0, 1, 2)):
        turns = {3: (0,), 4: (1, 3), 5: (2,)}.get(number, ())
        for part in parts:
            for copy in self.ring(part, number // 2, number % 2):
                copy.wait()
            if number < 5:
                self.post(part, number + 1)
            for turn in turns:
                self.pair(part, turn).start()

    def end(self, parts, turns=range(SIDE)):
        for part in parts:
            for turn in turns:
                self.pair(part, turn).wait()


def layer_kernel(
    n, scale, x, b, c, steps_t, cot, shard, out, grad_x, grad_b, grad_c,
    level, level_t, masked, masked_t, b_t, c_t, decays, y, send, near, joint, recv, stage, got, give, before, mixed,
    whole, back, dshift, flow, inner_sum, b_sum, c_sum, send2, near2, joint2, recv2, stage2, got2, give2, after,
    falls, tails, shifts,
    sems, own_sem, ring_send, ring_recv, pair_send, pair_recv,
):
    me = lax.axis_index("ctx")
    rows = x.shape[0]
    state = b.shape[1]
    core, chip, chips = lax.rem(me, 2), me // 2, n // 2
    partner = me + 1 - 2 * core
    first = (1 - core).astype(F32)
    second = 1.0 - first
    barrier = greet_all(n)
    gather = Gather(shard, whole, own_sem, ring_send, ring_recv, pair_send, pair_recv)
    pl.semaphore_wait(barrier, n // 2 + 2)
    gather.begin()

    accumulate_decay(steps_t, level_t)
    level[...] = flip(level_t[...])
    row, column = grid_of(rows, rows)
    masked[...] = jnp.where(row >= column, scale * dot_nt(c[...], b[...]), 0.0)
    masked_t[...] = jnp.where(row <= column, scale * dot_nt(b[...], c[...]), 0.0)
    b_t[...] = flip(b[...]).astype(BF)
    c_t[...] = flip(c[...]).astype(BF)
    inner_sum[...] = jnp.zeros_like(inner_sum)
    b_sum[...] = jnp.zeros_like(b_sum)
    c_sum[...] = jnp.zeros_like(c_sum)

    def make_term(q, carry):
        both, last = spread(level, q)
        falls[q] = jnp.exp2(-both)
        tail = jnp.exp2(both - last)
        tails[q] = tail
        shifted = (x[:, span(q, WIDE)].astype(F32) * tail).astype(BF)
        shifts[:, span(q, WIDE)] = shifted
        term = dot(b_t[...], shifted).astype(BF)
        parts = in_parts(jnp.exp2(-last))
        for u in range(2):
            send[u, q, :state] = term[:, u * LANES : (u + 1) * LANES]
            send[u, q, state:] = parts[:, u * LANES : (u + 1) * LANES]
        return carry

    def inside(q, carry):
        columns = columns_of(level, q)
        for u in range(2):
            mix = []
            for v in (2 * u, 2 * u + 1):
                gap = level_t[pl.ds(4 * q + v, 1), :] - columns[v]
                mix.append((masked[...] * jnp.exp2(jnp.minimum(gap, 0.0))).astype(BF))
            y[2 * q + u] = dot(jnp.concatenate(mix, axis=1), split_heads(x[:, span(2 * q + u)]))
        return carry

    gather.advance(0)
    lax.fori_loop(0, n // 8, make_term, 0)
    gather.advance(1)
    lax.fori_loop(n // 8, n // 2, make_term, 0)
    near_terms = copy_to(partner, send.at[1 - core], near, sems, 0)
    near_terms.start()
    gather.advance(2)
    lax.fori_loop(0, n // 8, inside, 0)
    gather.advance(3)
    near_terms.wait()

    def combine(q, carry):
        mine, theirs = from_parts(send[core, q, state:]), from_parts(near[q, state:])
        here = (first * theirs + second) * send[core, q, :state].astype(F32)
        there = (second * mine + first) * near[q, :state].astype(F32)
        joint[q, :state] = (here + there).astype(BF)
        joint[q, state:] = in_parts(mine * theirs)
        return carry

    lax.fori_loop(0, chips, combine, 0)

    def post_term(i, carry):
        q = lax.rem(chip + i, chips)
        copy_to(2 * q + core, joint.at[q], recv.at[chip], sems, 2).start()
        return carry

    lax.fori_loop(1, chips, post_term, 0)
    recv[chip] = joint[chip]
    lax.fori_loop(n // 8, n // 2, inside, 0)
    gather.advance(4, (0, 1))
    finish(n, joint, recv, sems, 2)

    def step(g, carry):
        for u in range(GROUP):
            k = g * GROUP + u
            stage[k] = carry.astype(BF)
            d = from_parts(recv[k, state:])
            decays[k] = jnp.broadcast_to(d, (8, LANES))
            carry = d * carry + recv[k, :state].astype(F32)

        def post(k, nothing):
            @pl.when(k != chip)
            def _():
                copy_to(2 * k + core, stage.at[k], got.at[chip], sems, 4).start()

            return nothing

        lax.fori_loop(g * GROUP, (g + 1) * GROUP, post, 0)
        return carry

    lax.fori_loop(0, chips // GROUP, step, jnp.zeros((state, LANES), F32))
    got[chip] = stage[chip]
    gather.advance(5, (0, 1))
    gather.advance(4, (2,))
    gather.end((0, 1))

    def place(i):
        row = i // SIDE
        turn = row + (row // 2) * (5 - 2 * row)
        return lax.rem(lax.axis_index("dp") + turn, SIDE) * SIDE + lax.rem(i, SIDE)

    early, late = pl.ds(0, CUTS[2]), pl.ds(CUTS[2], CUTS[3] - CUTS[2])

    def share(q, columns):
        chunk = whole[q // SIDE, lax.rem(q, SIDE), :, :, :, columns]
        return dot_nt(cot[:, columns], chunk.reshape(WIDE, chunk.shape[-1]))

    def begin_back(q, carry):
        part = share(q, early)
        for u in range(2):
            flow[2 * q + u] = part[:, u * LANES : (u + 1) * LANES]
        return carry

    lax.fori_loop(0, n // 2, begin_back, 0)
    finish(n, stage, got, sems, 4)

    def pass_on(q, carry):
        early_state = got[q].astype(F32)
        d = first * from_parts(send[core, q, state:]) + second * from_parts(near[q, state:])
        term = first * send[core, q, :state].astype(F32) + second * near[q, :state].astype(F32)
        late_state = d * early_state + term
        before[core, q] = (first * early_state + second * late_state).astype(BF)
        give[q] = (first * late_state + second * early_state).astype(BF)
        return carry

    lax.fori_loop(0, chips, pass_on, 0)
    near_states = copy_to(partner, give, before.at[core], sems, 6)
    near_states.start()
    gather.end((2,), (0, 1, 3))

    def make_back(i):
        q = place(i)
        back[:, span(q, WIDE)] = (beside(flow, q) + share(q, late)).astype(BF)

    def make_term_back(i):
        q = place(i)
        shift = (back[:, span(q, WIDE)].astype(F32) * falls[q]).astype(BF)
        dshift[:, span(q, WIDE)] = shift
        term = dot(c_t[...], shift).astype(BF)
        for u in range(2):
            send2[u, q] = term[:, u * LANES : (u + 1) * LANES]

    def post_back(i):
        q = place(i)
        copy_to(partner, send2.at[1 - core, q], near2.at[q], sems, 8).start()

    def send_term(i, carry):
        make_term_back(i - 1)
        make_back(i)
        post_back(i - 1)
        return carry

    make_back(0)
    lax.fori_loop(1, 2 * SIDE, send_term, 0)
    gather.advance(5, (2,))
    lax.fori_loop(2 * SIDE, 3 * SIDE, send_term, 0)
    gather.end((2,), (2,))
    lax.fori_loop(3 * SIDE, n // 2, send_term, 0)
    make_term_back(n // 2 - 1)
    post_back(n // 2 - 1)
    copy_to(partner, send2.at[1 - core], near2, sems, 8).wait()

    def combine_back(i, carry):
        q = lax.rem(chip + 1 + i, chips)
        mine, theirs = from_parts(send[core, q, state:]), from_parts(near[q, state:])
        here = (first + second * theirs) * send2[core, q].astype(F32)
        there = (first * mine + second) * near2[q].astype(F32)
        joint2[q] = (here + there).astype(BF)

        @pl.when(q != chip)
        def _():
            copy_to(2 * q + core, joint2.at[q], recv2.at[chip], sems, 10).start()

        return carry

    lax.fori_loop(0, chips, combine_back, 0)
    recv2[chip] = joint2[chip]
    near_states.wait()

    def inside_back(q, carry):
        columns = columns_of(level, q)
        total = inner_sum[...]
        for u in range(2):
            j = 2 * q + u
            part = back[:, span(j)]
            pair = dot_nt(split_heads(x[:, span(j)]), part)
            mix = []
            for v in range(2):
                gap = columns[2 * u + v] - level_t[pl.ds(4 * q + 2 * u + v, 1), :]
                fade = jnp.exp2(jnp.minimum(gap, 0.0))
                mix.append((masked_t[...] * fade).astype(BF))
                total = total + fade * pair[v * rows : (v + 1) * rows]
            flow[j] = dot(jnp.concatenate(mix, axis=1), split_heads(part))
        inner_sum[...] = total
        c_sum[...] += dot_nt(dshift[:, span(q, WIDE)], both_of(before, q))
        return carry

    held = n // 2 - 5
    lax.fori_loop(0, held, inside_back, 0)
    finish(n, joint2, recv2, sems, 10)

    def step_back(g, carry):
        for u in range(GROUP):
            k = chips - 1 - (g * GROUP + u)
            stage2[k] = carry.astype(BF)
            carry = decays[k, 0:1] * carry + recv2[k].astype(F32)

        def post(i, nothing):
            k = chips - 1 - i

            @pl.when(k != chip)
            def _():
                copy_to(2 * k + core, stage2.at[k], got2.at[chip], sems, 12).start()

            return nothing

        lax.fori_loop(g * GROUP, (g + 1) * GROUP, post, 0)
        return carry

    lax.fori_loop(0, chips // GROUP, step_back, jnp.zeros((state, LANES), F32))
    got2[chip] = stage2[chip]
    lax.fori_loop(held, n // 2, inside_back, 0)

    def join(q, carry):
        carried = scale * falls[q] * dot(c[...], both_of(before, q))
        mixed[:, span(q, WIDE)] = (beside(y, q) + carried).astype(BF)
        return carry

    lax.fori_loop(0, n // 2, join, 0)

    def project(i, carry):
        chunk = whole[:, :, :, :, :, span(i, WIDE)].reshape(x.shape[1], WIDE)
        out[:, span(i, WIDE)] = dot(mixed[...], chunk).astype(BF)
        return carry

    tiles = out.shape[1] // WIDE
    lax.fori_loop(0, 2, project, 0)
    finish(n, stage2, got2, sems, 12)

    def pass_back(q, carry):
        late_state = got2[q].astype(F32)
        d = first * from_parts(near[q, state:]) + second * from_parts(send[core, q, state:])
        term = first * near2[q].astype(F32) + second * send2[core, q].astype(F32)
        early_state = d * late_state + term
        after[core, q] = (first * early_state + second * late_state).astype(BF)
        give2[q] = (first * late_state + second * early_state).astype(BF)
        return carry

    lax.fori_loop(0, chips, pass_back, 0)
    near_after = copy_to(partner, give2, after.at[core], sems, 14)
    near_after.start()

    lax.fori_loop(2, tiles, project, 0)
    kernel_t = jnp.where(row <= column, scale * inner_sum[...], 0.0)
    kernel = kernel_t.T.astype(BF)
    grad_c[...] = (dot(kernel, b[...]) + scale * c_sum[...]).astype(BF)
    near_after.wait()

    def join_back(q, carry):
        late = both_of(after, q)
        carried = scale * tails[q] * dot(b[...], late)
        grad_x[:, span(q, WIDE)] = (beside(flow, q) + carried).astype(BF)
        b_sum[...] += dot_nt(shifts[:, span(q, WIDE)], late)
        return carry

    lax.fori_loop(0, n // 2, join_back, 0)
    grad_b[...] = (dot(kernel_t.astype(BF), c[...]) + scale * b_sum[...]).astype(BF)


def body(x_in, b_in, c_in, log_decay, w_out, cotangent):
    x, b, c, steps, cot = x_in[0], b_in[0], c_in[0], log_decay[0], cotangent[0]
    rows = x.shape[0]
    state = b.shape[1]
    n = lax.axis_size("ctx")
    scale = (state * rows * n) ** (-0.5)
    vmem = pl.BlockSpec(memory_space=pltpu.VMEM)
    shape = jax.ShapeDtypeStruct
    square = pltpu.VMEM((rows, rows), F32)
    turned = pltpu.VMEM((state, rows), BF)
    blocks = pltpu.VMEM((n // 2, state, LANES), BF)
    marked = pltpu.VMEM((n // 2, state + 16, LANES), BF)
    slabs = pltpu.VMEM((2, n // 2, state, LANES), BF)
    marked_slabs = pltpu.VMEM((2, n // 2, state + 16, LANES), BF)
    parts = pltpu.VMEM((n, rows, LANES), F32)
    wide = pltpu.VMEM(x.shape, BF)
    spreads = pltpu.VMEM((n // 2, rows, WIDE), F32)
    sums = pltpu.VMEM((rows, state), F32)
    ring = pltpu.SemaphoreType.DMA((3, 3, 2, 2))
    pair = pltpu.SemaphoreType.DMA((3, SIDE))
    results = pl.pallas_call(
        functools.partial(layer_kernel, n, scale),
        out_shape=(
            shape(cot.shape, BF), shape(x.shape, BF), shape(b.shape, BF), shape(c.shape, BF),
        ),
        in_specs=[vmem] * 6,
        out_specs=(vmem,) * 4,
        scratch_shapes=[
            square, square, square, square, turned, turned,
            pltpu.VMEM((n // 2, 8, LANES), F32),
            parts, marked_slabs, marked, marked, marked, blocks, blocks, blocks, slabs, wide,
            pltpu.VMEM((SIDE, SIDE, SIDE, 2) + w_out.shape, BF),
            wide, wide, parts, square, sums, sums,
            slabs, blocks, blocks, blocks, blocks, blocks, blocks, slabs,
            spreads, spreads, wide,
            pltpu.SemaphoreType.DMA((16,)),
            pltpu.SemaphoreType.DMA((1,)),
            ring, ring, pair, pair,
        ],
        compiler_params=pltpu.CompilerParams(
            collective_id=0, has_side_effects=True, vmem_limit_bytes=60 * 1024 * 1024
        ),
        name="layer",
    )(x, b, c, steps.T, cot, w_out)
    return tuple(r[None] for r in results)


def solution(mesh):
    tokens = P("dp", "ctx", None)
    return jax.shard_map(
        body,
        mesh=mesh,
        in_specs=(tokens, tokens, tokens, tokens, P(("dp", "ctx"), None), tokens),
        out_specs=(tokens, tokens, tokens, tokens),
        check_vma=False,
    )
```
